256 devices in a mesh: dp: 64 (over z, y, core), sub: 4 (over x).
Axes of the slice: x: 4, y: 4, z: 8, core: 2. Of those that a mesh axis runs over, the one named last changes fastest.
Arguments:
- partials: float32 [64, 96, 64, 1024], P('dp', None, None, 'sub'), may hold values from -6 to 6
- owner: int32 [96], replicated, may hold values from 0 to 63, as said below
- basis_old: float32 [4, 1024, 256], P(None, 'sub'), may hold values from -0.1875 to 0.1875
- moment1: float32 [128, 64, 256], P('dp', 'sub'), may hold values from -4 to 4
- moment2: float32 [128, 64, 256], P('dp', 'sub'), may hold values from 0.01 to 1
- master: bfloat16 [128, 64, 1024], P('dp', None, 'sub'), may hold values from -0.1875 to 0.1875
Outputs:
- weights: bfloat16 [96, 64, 1024], P(None, None, 'sub')
- basis_new: float32 [4, 1024, 256], P(None, 'sub')
- moment1_new: float32 [128, 64, 256], P('dp', 'sub')
- moment2_new: float32 [128, 64, 256], P('dp', 'sub')
The draws below stay inside these ranges and needn't reach their ends.
Inputs may be any that keep to these rules, and one draw needn't show every extreme that they name: `owner`: each index of dp owns at least one block and at most 2 blocks, and some index owns exactly 2.
All inputs are finite; a program needn't handle non-finite values.
Results may differ from the reference program's by a relative error of at most 0.0095.
Values may be sent and summed in bfloat16 or wider, within the bound.
A program may use at most 64 MiB of HBM per device.

```python
import math
import jax
import jax.numpy as jnp
from jax import lax

D = 1024
VW = 2048
RANK = 256
BW = 64
NS_ITERS = 5
NMAT = 4
NB = 96
SLOTS = 2
N_DP = 64


def draw_owner(key, part):
    first_key = jax.random.fold_in(key, 11)
    extra_key = jax.random.fold_in(key, 23)
    order_key = jax.random.fold_in(key, 37)
    firsts = jax.random.permutation(first_key, N_DP).astype(jnp.int32)
    if NB > N_DP:
        extra_slots = jax.random.permutation(extra_key, N_DP * (SLOTS - 1))
        extras = (extra_slots[:NB - N_DP] // (SLOTS - 1)).astype(jnp.int32)
        owners = jnp.concatenate([firsts, extras])
    else:
        owners = firsts
    order = jax.random.permutation(order_key, NB)
    return owners[order].astype(jnp.int32)


def steps_of(own_key, extent, cuts, least, top_value):
    level = 1.0
    for position, blocks in cuts:
        heights = jax.random.uniform(jax.random.fold_in(jax.random.fold_in(own_key, 6), position), (blocks,), jnp.float32, least / len(cuts), top_value / len(cuts))
        level = level * jnp.repeat(jnp.exp(heights), extent[position] // blocks).reshape((-1,) + (1,) * (len(extent) - 1 - position))
    return level


def normal_values(key, extent, width, reach, cuts=(), kind=jnp.bfloat16):
    entries = width * jax.random.normal(key, extent, jnp.float32)
    if cuts:
        entries = entries * steps_of(key, extent, cuts, -0.22, 0.18)
    return jnp.clip(entries, -reach, reach).astype(kind)


def setup_inputs(seed: int = 0) -> dict:
    key_list = jax.random.split(jax.random.key(seed), 7)
    return {
        "partials": normal_values(key_list[0], (N_DP, NB, BW, D), 1.0, 6.0, ((0, 64), (3, 4)), jnp.float32),
        "owner": draw_owner(jax.random.fold_in(key_list[6], 71), 0),
        "basis_old": normal_values(key_list[2], (NMAT, D, RANK), D ** -0.5, 0.1875, ((1, 4),), jnp.float32),
        "moment1": normal_values(key_list[3], (N_DP * SLOTS, BW, RANK), 0.25, 4.0, ((0, 64), (1, 4)), jnp.float32),
        "moment2": jnp.clip(jnp.exp(math.log(1.0) - 4.6051702 * jax.random.uniform(key_list[4], (N_DP * SLOTS, BW, RANK), jnp.float32) ** steps_of(key_list[4], (N_DP * SLOTS, BW, RANK), ((0, 64), (1, 4)), -0.2, 0.2)), 0.01, 1.0),
        "master": normal_values(key_list[5], (N_DP * SLOTS, BW, D), D ** -0.5, 0.1875, ((0, 64), (2, 4))),
    }


HIGH = lax.Precision.HIGHEST
BETA_ONE = 0.9
BETA_TWO = 0.999
CORR_ONE = 1.0 - 0.9 ** 10
CORR_TWO = 1.0 - 0.999 ** 10
LEARN = 0.05
TINY = 1e-08
NORM_EPS = 1e-06

def matrix_index(block_ids):
    q_blocks = D // BW
    v_blocks = VW // BW
    first = (block_ids >= q_blocks).astype(jnp.int32)
    second = (block_ids >= 2 * q_blocks).astype(jnp.int32)
    third = (block_ids >= 2 * q_blocks + v_blocks).astype(jnp.int32)
    return first + second + third

def reference(partials, owner, basis_old, moment1, moment2, master):
    grad = lax.optimization_barrier(jnp.sum(partials, axis=0))
    count = grad.shape[0]
    block_ids = jnp.arange(count, dtype=jnp.int32)
    matrix_of = matrix_index(block_ids)
    same_owner = owner[:, None] == owner[None, :]
    earlier = block_ids[None, :] < block_ids[:, None]
    rank_within = lax.optimization_barrier(jnp.sum((same_owner & earlier).astype(jnp.int32), axis=1)).astype(jnp.int32)
    slot_of = (owner * SLOTS + rank_within).astype(jnp.int32)
    old_each = basis_old[matrix_of]
    crossed = jnp.einsum('bcd,bdr->bcr', grad, old_each, precision=HIGH)
    refresh_term = jnp.einsum('bcd,bcr->bdr', grad, crossed, precision=HIGH)
    matrix_hits = (matrix_of[:, None] == jnp.arange(NMAT, dtype=jnp.int32)[None, :]).astype(jnp.float32)
    refresh = jnp.einsum('bm,bdr->mdr', matrix_hits, refresh_term, precision=HIGH)
    basis = refresh / jnp.sqrt(lax.optimization_barrier(jnp.sum(refresh * refresh, axis=(1, 2))) + NORM_EPS)[:, None, None]
    for sweep in range(NS_ITERS):
        gram_mat = jnp.einsum('mdr,mds->mrs', basis, basis, precision=HIGH)
        basis = 1.5 * basis - 0.5 * jnp.einsum('mdr,mrs->mds', basis, gram_mat, precision=HIGH)
    new_each = basis[matrix_of]
    projected = jnp.einsum('bcd,bdr->bcr', grad, new_each, precision=HIGH)
    first_new = BETA_ONE * moment1[slot_of] + (1.0 - BETA_ONE) * projected
    second_new = BETA_TWO * moment2[slot_of] + (1.0 - BETA_TWO) * projected * projected
    adam_step = first_new / CORR_ONE / (jnp.sqrt(second_new / CORR_TWO) + TINY)
    update = jnp.einsum('bcr,bdr->bcd', adam_step, new_each, precision=HIGH)
    weights = (master[slot_of].astype(jnp.float32) - LEARN * update).astype(jnp.bfloat16)
    moment1_new = jnp.zeros(moment1.shape, jnp.float32).at[slot_of].set(first_new)
    moment2_new = jnp.zeros(moment2.shape, jnp.float32).at[slot_of].set(second_new)
    return (weights, basis, moment1_new, moment2_new)
```

```python
import jax
import jax.numpy as jnp
from jax import lax
from jax.sharding import PartitionSpec as P

D = 1024
VW = 2048
BW = 64
NS_ITERS = 5
NMAT = 4


HIGH = lax.Precision.HIGHEST
BETA_ONE = 0.9
BETA_TWO = 0.999
CORR_ONE = 1.0 - 0.9**10
CORR_TWO = 1.0 - 0.999**10
LEARN = 0.05
TINY = 1e-08
NORM_EPS = 1e-06


def matrix_index(block_ids):
    q_blocks = D // BW
    v_blocks = VW // BW
    first = (block_ids >= q_blocks).astype(jnp.int32)
    second = (block_ids >= 2 * q_blocks).astype(jnp.int32)
    third = (block_ids >= 2 * q_blocks + v_blocks).astype(jnp.int32)
    return first + second + third


def local(partials, owner, basis_old, moment1, moment2, master):
    local_grad = partials[0]
    count = local_grad.shape[0]
    n_data = lax.axis_size("dp")
    slots = moment1.shape[0]
    total_slots = n_data * slots
    my_index = lax.axis_index("dp")
    block_ids = jnp.arange(count, dtype=jnp.int32)
    same_owner = owner[:, None] == owner[None, :]
    earlier = block_ids[None, :] < block_ids[:, None]
    rank_within = jnp.sum((same_owner & earlier).astype(jnp.int32), axis=1)
    slot_of = owner * slots + rank_within
    slot_ids = jnp.arange(total_slots, dtype=jnp.int32)
    slot_hits = slot_of[None, :] == slot_ids[:, None]
    filled = jnp.any(slot_hits, axis=1)
    slot_block = jnp.sum(jnp.where(slot_hits, block_ids[None, :], 0), axis=1)
    sendbuf = jnp.where(filled[:, None, None], jnp.take(local_grad, slot_block, axis=0), 0.0)
    owned_grad = lax.psum_scatter(sendbuf, "dp", scatter_dimension=0, tiled=True)
    my_blocks = lax.dynamic_slice_in_dim(slot_block, my_index * slots, slots)
    my_filled = lax.dynamic_slice_in_dim(filled, my_index * slots, slots)
    my_matrix = matrix_index(my_blocks)
    old_each = jnp.take(basis_old, my_matrix, axis=0)
    crossed = lax.psum(
        jnp.einsum("scd,sdr->scr", owned_grad, old_each, precision=HIGH).astype(jnp.bfloat16), "sub"
    ).astype(jnp.float32)
    refresh_term = jnp.einsum("scd,scr->sdr", owned_grad, crossed, precision=HIGH)
    matrix_hits = (
        (my_matrix[:, None] == jnp.arange(NMAT, dtype=jnp.int32)[None, :]) & my_filled[:, None]
    ).astype(jnp.float32)
    local_refresh = jnp.einsum("sm,sdr->mdr", matrix_hits, refresh_term, precision=HIGH)
    refresh = lax.psum(local_refresh, "dp")
    refresh_each = jnp.take(refresh, my_matrix, axis=0)
    n_mat, rows, rank = refresh.shape
    gram_part = jnp.einsum("mdr,mds->mrs", refresh, refresh, precision=HIGH)
    cross_part = jnp.einsum("scd,sdr->scr", owned_grad, refresh_each, precision=HIGH)
    joined = jnp.concatenate(
        [gram_part.reshape(n_mat * rank, rank), cross_part.reshape(-1, rank)], axis=0
    )
    joined = lax.psum(joined, "sub")
    gram = joined[: n_mat * rank].reshape(n_mat, rank, rank)
    cross = joined[n_mat * rank :].reshape(cross_part.shape)
    norm_sq = jnp.trace(gram, axis1=1, axis2=2) + NORM_EPS
    g0 = gram / norm_sq[:, None, None]
    eye = jnp.broadcast_to(jnp.eye(rank, dtype=jnp.float32), g0.shape)
    poly = 1.5 * eye - 0.5 * g0
    for sweep in range(1, NS_ITERS):
        inner = jnp.einsum("mst,mtu->msu", g0, poly, precision=HIGH)
        h = jnp.einsum("msr,msu->mru", poly, inner, precision=HIGH)
        poly = 1.5 * poly - 0.5 * jnp.einsum("mrs,msu->mru", poly, h, precision=HIGH)
    inv_norm = 1.0 / jnp.sqrt(norm_sq)
    basis = jnp.einsum("mdr,mrs->mds", refresh, poly, precision=HIGH) * inv_norm[:, None, None]
    new_each = jnp.take(basis, my_matrix, axis=0)
    poly_each = jnp.take(poly, my_matrix, axis=0)
    projected_all = jnp.einsum("scr,sru->scu", cross, poly_each, precision=HIGH) * jnp.take(
        inv_norm, my_matrix
    )[:, None, None]
    rows_here = moment1.shape[1]
    projected = lax.dynamic_slice_in_dim(
        projected_all, lax.axis_index("sub") * rows_here, rows_here, axis=1
    )
    first_new = BETA_ONE * moment1 + (1.0 - BETA_ONE) * projected
    second_new = BETA_TWO * moment2 + (1.0 - BETA_TWO) * projected * projected
    adam_step = first_new / CORR_ONE / (jnp.sqrt(second_new / CORR_TWO) + TINY)
    full_step = lax.all_gather(adam_step.astype(jnp.bfloat16), "sub", axis=1, tiled=True).astype(
        adam_step.dtype
    )
    update = jnp.einsum("scr,sdr->scd", full_step, new_each, precision=HIGH)
    new_master = (master.astype(jnp.float32) - LEARN * update).astype(jnp.bfloat16)
    every_slot = lax.all_gather(new_master, "dp", axis=0, tiled=True)
    weights = jnp.take(every_slot, slot_of, axis=0)
    moment1_new = jnp.where(my_filled[:, None, None], first_new, 0.0)
    moment2_new = jnp.where(my_filled[:, None, None], second_new, 0.0)
    return (weights, basis, moment1_new, moment2_new)


def solution(mesh):
    return jax.shard_map(
        local,
        mesh=mesh,
        in_specs=(
            P("dp", None, None, "sub"),
            P(),
            P(None, "sub", None),
            P("dp", "sub", None),
            P("dp", "sub", None),
            P("dp", None, "sub"),
        ),
        out_specs=(
            P(None, None, "sub"),
            P(None, "sub", None),
            P("dp", "sub", None),
            P("dp", "sub", None),
        ),
        check_vma=False,
    )
```

```python
import jax
import jax.numpy as jnp
from jax import lax
from jax.sharding import PartitionSpec as P

D = 1024
VW = 2048
BW = 64
NS_ITERS = 5
NMAT = 4


HIGH = lax.Precision.HIGHEST
BETA_ONE = 0.9
BETA_TWO = 0.999
CORR_ONE = 1.0 - 0.9**10
CORR_TWO = 1.0 - 0.999**10
LEARN = 0.05
TINY = 1e-08
NORM_EPS = 1e-06


def matrix_index(block_ids):
    q_blocks = D // BW
    v_blocks = VW // BW
    first = (block_ids >= q_blocks).astype(jnp.int32)
    second = (block_ids >= 2 * q_blocks).astype(jnp.int32)
    third = (block_ids >= 2 * q_blocks + v_blocks).astype(jnp.int32)
    return first + second + third


def butterfly_sum(x, axis):
    size = lax.axis_size(axis)
    for bit in range(size.bit_length() - 1):
        pairs = [(i, i ^ (1 << bit)) for i in range(size)]
        x = x + lax.ppermute(x, axis, pairs)
    return x


def doubling_gather(x, axis, bits):
    size = lax.axis_size(axis)
    for bit in bits:
        pairs = [(i, i ^ (1 << bit)) for i in range(size)]
        x = jnp.concatenate([x, lax.ppermute(x, axis, pairs)], axis=0)
    return x


def local(partials, owner, basis_old, moment1, moment2, master):
    local_grad = partials[0]
    count = local_grad.shape[0]
    n_data = lax.axis_size("dp")
    slots = moment1.shape[0]
    total_slots = n_data * slots
    my_index = lax.axis_index("dp")
    block_ids = jnp.arange(count, dtype=jnp.int32)
    same_owner = owner[:, None] == owner[None, :]
    earlier = block_ids[None, :] < block_ids[:, None]
    rank_within = jnp.sum((same_owner & earlier).astype(jnp.int32), axis=1)
    slot_of = owner * slots + rank_within
    slot_ids = jnp.arange(total_slots, dtype=jnp.int32)
    slot_hits = slot_of[None, :] == slot_ids[:, None]
    filled = jnp.any(slot_hits, axis=1)
    slot_block = jnp.sum(jnp.where(slot_hits, block_ids[None, :], 0), axis=1)
    sendbuf = jnp.where(filled[:, None, None], jnp.take(local_grad, slot_block, axis=0), 0.0)
    owned_grad = lax.psum_scatter(sendbuf, "dp", scatter_dimension=0, tiled=True)
    my_blocks = lax.dynamic_slice_in_dim(slot_block, my_index * slots, slots)
    my_filled = lax.dynamic_slice_in_dim(filled, my_index * slots, slots)
    my_matrix = matrix_index(my_blocks)
    old_each = jnp.take(basis_old, my_matrix, axis=0)
    crossed = butterfly_sum(
        jnp.einsum("scd,sdr->scr", owned_grad, old_each, precision=HIGH), "sub"
    )
    refresh_term = jnp.einsum("scd,scr->sdr", owned_grad, crossed, precision=HIGH)
    matrix_hits = (
        (my_matrix[:, None] == jnp.arange(NMAT, dtype=jnp.int32)[None, :]) & my_filled[:, None]
    ).astype(jnp.float32)
    local_refresh = jnp.einsum("sm,sdr->mdr", matrix_hits, refresh_term, precision=HIGH)
    refresh = butterfly_sum(local_refresh, "dp")
    refresh_each = jnp.take(refresh, my_matrix, axis=0)
    n_mat, rows, rank = refresh.shape
    gram_part = jnp.einsum("mdr,mds->mrs", refresh, refresh, precision=HIGH)
    cross_part = jnp.einsum("scd,sdr->scr", owned_grad, refresh_each, precision=HIGH)
    joined = jnp.concatenate(
        [gram_part.reshape(n_mat * rank, rank), cross_part.reshape(-1, rank)], axis=0
    )
    joined = butterfly_sum(joined, "sub")
    gram = joined[: n_mat * rank].reshape(n_mat, rank, rank)
    cross = joined[n_mat * rank :].reshape(cross_part.shape)
    norm_sq = jnp.trace(gram, axis1=1, axis2=2) + NORM_EPS
    g0 = gram / norm_sq[:, None, None]
    eye = jnp.broadcast_to(jnp.eye(rank, dtype=jnp.float32), g0.shape)
    poly = 1.5 * eye - 0.5 * g0
    for sweep in range(1, NS_ITERS):
        inner = jnp.einsum("mst,mtu->msu", g0, poly, precision=HIGH)
        h = jnp.einsum("msr,msu->mru", poly, inner, precision=HIGH)
        poly = 1.5 * poly - 0.5 * jnp.einsum("mrs,msu->mru", poly, h, precision=HIGH)
    inv_norm = 1.0 / jnp.sqrt(norm_sq)
    basis = jnp.einsum("mdr,mrs->mds", refresh, poly, precision=HIGH) * inv_norm[:, None, None]
    new_each = jnp.take(basis, my_matrix, axis=0)
    poly_each = jnp.take(poly, my_matrix, axis=0)
    projected_all = jnp.einsum("scr,sru->scu", cross, poly_each, precision=HIGH) * jnp.take(
        inv_norm, my_matrix
    )[:, None, None]
    rows_here = moment1.shape[1]
    projected = lax.dynamic_slice_in_dim(
        projected_all, lax.axis_index("sub") * rows_here, rows_here, axis=1
    )
    first_new = BETA_ONE * moment1 + (1.0 - BETA_ONE) * projected
    second_new = BETA_TWO * moment2 + (1.0 - BETA_TWO) * projected * projected
    adam_step = first_new / CORR_ONE / (jnp.sqrt(second_new / CORR_TWO) + TINY)
    full_step = lax.all_gather(adam_step.astype(jnp.bfloat16), "sub", axis=1, tiled=True).astype(
        adam_step.dtype
    )
    update = jnp.einsum("scr,sdr->scd", full_step, new_each, precision=HIGH)
    new_master = (master.astype(jnp.float32) - LEARN * update).astype(jnp.bfloat16)
    n_bits = n_data.bit_length() - 1
    order = list(range(n_bits))[::-1]
    every_slot = doubling_gather(new_master, "dp", order)
    apart = my_index ^ owner
    place = sum(((apart >> bit) & 1) << step for step, bit in enumerate(order))
    weights = jnp.take(every_slot, place * slots + rank_within, axis=0)
    moment1_new = jnp.where(my_filled[:, None, None], first_new, 0.0)
    moment2_new = jnp.where(my_filled[:, None, None], second_new, 0.0)
    return (weights, basis, moment1_new, moment2_new)


def solution(mesh):
    return jax.shard_map(
        local,
        mesh=mesh,
        in_specs=(
            P("dp", None, None, "sub"),
            P(),
            P(None, "sub", None),
            P("dp", "sub", None),
            P("dp", "sub", None),
            P("dp", None, "sub"),
        ),
        out_specs=(
            P(None, None, "sub"),
            P(None, "sub", None),
            P("dp", "sub", None),
            P("dp", "sub", None),
        ),
        check_vma=False,
    )
```

```python
import jax
import jax.numpy as jnp
from jax import lax
from jax.sharding import PartitionSpec as P

D = 1024
VW = 2048
BW = 64
NS_ITERS = 5
NMAT = 4


HIGH = lax.Precision.HIGHEST
BETA_ONE = 0.9
BETA_TWO = 0.999
CORR_ONE = 1.0 - 0.9**10
CORR_TWO = 1.0 - 0.999**10
LEARN = 0.05
TINY = 1e-08
NORM_EPS = 1e-06


def matrix_index(block_ids):
    q_blocks = D // BW
    v_blocks = VW // BW
    first = (block_ids >= q_blocks).astype(jnp.int32)
    second = (block_ids >= 2 * q_blocks).astype(jnp.int32)
    third = (block_ids >= 2 * q_blocks + v_blocks).astype(jnp.int32)
    return first + second + third


def butterfly_sum(x, axis):
    size = lax.axis_size(axis)
    for bit in range(size.bit_length() - 1):
        pairs = [(i, i ^ (1 << bit)) for i in range(size)]
        x = x + lax.ppermute(x, axis, pairs)
    return x


def doubling_gather(x, axis, bits):
    size = lax.axis_size(axis)
    for bit in bits:
        pairs = [(i, i ^ (1 << bit)) for i in range(size)]
        x = jnp.concatenate([x, lax.ppermute(x, axis, pairs)], axis=0)
    return x


def halving_sum(x, axis, bits):
    index = lax.axis_index(axis)
    size = lax.axis_size(axis)
    for bit in bits:
        half = x.shape[0] // 2
        upper = ((index >> bit) & 1) == 1
        keep = jnp.where(upper, x[half:], x[:half])
        send = jnp.where(upper, x[:half], x[half:])
        pairs = [(i, i ^ (1 << bit)) for i in range(size)]
        x = keep + lax.ppermute(send, axis, pairs)
    return x


def doubling_merge(x, axis, bits):
    index = lax.axis_index(axis)
    size = lax.axis_size(axis)
    for bit in bits:
        upper = ((index >> bit) & 1) == 1
        pairs = [(i, i ^ (1 << bit)) for i in range(size)]
        got = lax.ppermute(x, axis, pairs)
        x = jnp.where(upper, jnp.concatenate([got, x], axis=0), jnp.concatenate([x, got], axis=0))
    return x


def rounded_butterfly_sum(x, axis):
    size = lax.axis_size(axis)
    for bit in range(size.bit_length() - 1):
        pairs = [(i, i ^ (1 << bit)) for i in range(size)]
        narrow = x.astype(jnp.bfloat16)
        x = narrow.astype(jnp.float32) + lax.ppermute(narrow, axis, pairs).astype(jnp.float32)
    return x


def local(partials, owner, basis_old, moment1, moment2, master):
    local_grad = partials[0]
    count = local_grad.shape[0]
    n_data = lax.axis_size("dp")
    slots = moment1.shape[0]
    total_slots = n_data * slots
    my_index = lax.axis_index("dp")
    block_ids = jnp.arange(count, dtype=jnp.int32)
    same_owner = owner[:, None] == owner[None, :]
    earlier = block_ids[None, :] < block_ids[:, None]
    rank_within = jnp.sum((same_owner & earlier).astype(jnp.int32), axis=1)
    slot_of = owner * slots + rank_within
    slot_ids = jnp.arange(total_slots, dtype=jnp.int32)
    slot_hits = slot_of[None, :] == slot_ids[:, None]
    filled = jnp.any(slot_hits, axis=1)
    slot_block = jnp.sum(jnp.where(slot_hits, block_ids[None, :], 0), axis=1)
    source = jnp.where(filled, slot_block, count)
    sendbuf = jnp.take(local_grad, source, axis=0, mode="fill", fill_value=0.0)
    owned_grad = lax.psum_scatter(sendbuf, "dp", scatter_dimension=0, tiled=True)
    my_blocks = lax.dynamic_slice_in_dim(slot_block, my_index * slots, slots)
    my_filled = lax.dynamic_slice_in_dim(filled, my_index * slots, slots)
    my_matrix = matrix_index(my_blocks)
    old_each = jnp.take(basis_old, my_matrix, axis=0)
    crossed = butterfly_sum(
        jnp.einsum("scd,sdr->scr", owned_grad, old_each, precision=HIGH), "sub"
    )
    refresh_term = jnp.einsum("scd,scr->sdr", owned_grad, crossed, precision=HIGH)
    matrix_hits = (
        (my_matrix[:, None] == jnp.arange(NMAT, dtype=jnp.int32)[None, :]) & my_filled[:, None]
    ).astype(jnp.float32)
    local_refresh = jnp.einsum("sm,sdr->mdr", matrix_hits, refresh_term, precision=HIGH)
    n_bits = n_data.bit_length() - 1
    link_order = [0, 1, 3, 2, 4, 5] if n_bits == 6 else list(range(n_bits))
    flat_refresh = local_refresh.reshape(-1, local_refresh.shape[-1])
    refresh = doubling_merge(
        halving_sum(flat_refresh, "dp", link_order), "dp", link_order[::-1]
    ).reshape(local_refresh.shape)
    refresh_each = jnp.take(refresh, my_matrix, axis=0)
    n_mat, rows, rank = refresh.shape
    gram_part = jnp.einsum("mdr,mds->mrs", refresh, refresh, precision=HIGH)
    cross_part = jnp.einsum("scd,sdr->scr", owned_grad, refresh_each, precision=HIGH)
    gram = rounded_butterfly_sum(gram_part, "sub")
    cross = butterfly_sum(cross_part, "sub")
    norm_sq = jnp.trace(gram, axis1=1, axis2=2) + NORM_EPS
    g0 = gram / norm_sq[:, None, None]
    eye = jnp.broadcast_to(jnp.eye(rank, dtype=jnp.float32), g0.shape)
    poly = 1.5 * eye - 0.5 * g0
    for sweep in range(1, NS_ITERS):
        inner = jnp.einsum("mst,mtu->msu", g0, poly, precision=HIGH)
        h = jnp.einsum("msr,msu->mru", poly, inner, precision=HIGH)
        poly = 1.5 * poly - 0.5 * jnp.einsum("mrs,msu->mru", poly, h, precision=HIGH)
    inv_norm = 1.0 / jnp.sqrt(norm_sq)
    basis = jnp.einsum("mdr,mrs->mds", refresh, poly, precision=HIGH) * inv_norm[:, None, None]
    new_each = jnp.take(basis, my_matrix, axis=0)
    poly_each = jnp.take(poly, my_matrix, axis=0)
    projected_all = jnp.einsum("scr,sru->scu", cross, poly_each, precision=HIGH) * jnp.take(
        inv_norm, my_matrix
    )[:, None, None]
    rows_here = moment1.shape[1]
    projected = lax.dynamic_slice_in_dim(
        projected_all, lax.axis_index("sub") * rows_here, rows_here, axis=1
    )
    first_new = BETA_ONE * moment1 + (1.0 - BETA_ONE) * projected
    second_new = BETA_TWO * moment2 + (1.0 - BETA_TWO) * projected * projected
    adam_step = first_new / CORR_ONE / (jnp.sqrt(second_new / CORR_TWO) + TINY)
    full_step = lax.all_gather(adam_step.astype(jnp.bfloat16), "sub", axis=1, tiled=True).astype(
        adam_step.dtype
    )
    update = jnp.einsum("scr,sdr->scd", full_step, new_each, precision=HIGH)
    new_master = (master.astype(jnp.float32) - LEARN * update).astype(jnp.bfloat16)
    order = list(range(n_bits))[::-1]
    every_slot = doubling_gather(new_master, "dp", order)
    apart = my_index ^ owner
    place = sum(((apart >> bit) & 1) << step for step, bit in enumerate(order))
    weights = jnp.take(every_slot, place * slots + rank_within, axis=0)
    moment1_new = jnp.where(my_filled[:, None, None], first_new, 0.0)
    moment2_new = jnp.where(my_filled[:, None, None], second_new, 0.0)
    return (weights, basis, moment1_new, moment2_new)


def solution(mesh):
    return jax.shard_map(
        local,
        mesh=mesh,
        in_specs=(
            P("dp", None, None, "sub"),
            P(),
            P(None, "sub", None),
            P("dp", "sub", None),
            P("dp", "sub", None),
            P("dp", None, "sub"),
        ),
        out_specs=(
            P(None, None, "sub"),
            P(None, "sub", None),
            P("dp", "sub", None),
            P("dp", "sub", None),
        ),
        check_vma=False,
    )
```

```python
import jax
import jax.numpy as jnp
from jax import lax
from jax.sharding import PartitionSpec as P

D = 1024
VW = 2048
BW = 64
NS_ITERS = 5
NMAT = 4


HIGH = lax.Precision.HIGHEST
BETA_ONE = 0.9
BETA_TWO = 0.999
CORR_ONE = 1.0 - 0.9**10
CORR_TWO = 1.0 - 0.999**10
LEARN = 0.05
TINY = 1e-08
NORM_EPS = 1e-06


def matrix_index(block_ids):
    q_blocks = D // BW
    v_blocks = VW // BW
    first = (block_ids >= q_blocks).astype(jnp.int32)
    second = (block_ids >= 2 * q_blocks).astype(jnp.int32)
    third = (block_ids >= 2 * q_blocks + v_blocks).astype(jnp.int32)
    return first + second + third


def butterfly_sum(x, axis):
    size = lax.axis_size(axis)
    for bit in range(size.bit_length() - 1):
        pairs = [(i, i ^ (1 << bit)) for i in range(size)]
        x = x + lax.ppermute(x, axis, pairs)
    return x


def doubling_gather(x, axis, bits):
    size = lax.axis_size(axis)
    for bit in bits:
        pairs = [(i, i ^ (1 << bit)) for i in range(size)]
        x = jnp.concatenate([x, lax.ppermute(x, axis, pairs)], axis=0)
    return x


def halving_sum(x, axis, bits):
    index = lax.axis_index(axis)
    size = lax.axis_size(axis)
    for bit in bits:
        half = x.shape[0] // 2
        upper = ((index >> bit) & 1) == 1
        keep = jnp.where(upper, x[half:], x[:half])
        send = jnp.where(upper, x[:half], x[half:])
        pairs = [(i, i ^ (1 << bit)) for i in range(size)]
        x = keep + lax.ppermute(send, axis, pairs)
    return x


def doubling_merge(x, axis, bits):
    index = lax.axis_index(axis)
    size = lax.axis_size(axis)
    for bit in bits:
        upper = ((index >> bit) & 1) == 1
        pairs = [(i, i ^ (1 << bit)) for i in range(size)]
        got = lax.ppermute(x, axis, pairs)
        x = jnp.where(upper, jnp.concatenate([got, x], axis=0), jnp.concatenate([x, got], axis=0))
    return x


def rounded_butterfly_sum(x, axis):
    size = lax.axis_size(axis)
    for bit in range(size.bit_length() - 1):
        pairs = [(i, i ^ (1 << bit)) for i in range(size)]
        narrow = x.astype(jnp.bfloat16)
        x = narrow.astype(jnp.float32) + lax.ppermute(narrow, axis, pairs).astype(jnp.float32)
    return x


def owner_scatter(local_grad, slot_block, axis, orders):
    index = lax.axis_index(axis)
    size = lax.axis_size(axis)
    slots = slot_block.shape[0] // size
    part = local_grad.shape[-1] // len(orders)
    position = jnp.arange(size, dtype=jnp.int32)
    pieces = []
    for k, order in enumerate(orders):
        steps = len(order)
        mask = sum(((position >> (steps - 1 - j)) & 1) << bit for j, bit in enumerate(order))
        dest = index ^ mask
        slot_index = (dest[:, None] * slots + jnp.arange(slots, dtype=jnp.int32)[None, :]).reshape(-1)
        columns = local_grad[..., k * part : (k + 1) * part]
        pieces.append(jnp.take(columns, jnp.take(slot_block, slot_index), axis=0))
    for j in range(len(orders[0])):
        for k, order in enumerate(orders):
            x = pieces[k]
            half = x.shape[0] // 2
            pairs = [(i, i ^ (1 << order[j])) for i in range(size)]
            pieces[k] = x[:half] + lax.ppermute(x[half:], axis, pairs)
    return jnp.concatenate(pieces, axis=-1)


def local(partials, owner, basis_old, moment1, moment2, master):
    local_grad = partials[0]
    count = local_grad.shape[0]
    n_data = lax.axis_size("dp")
    slots = moment1.shape[0]
    total_slots = n_data * slots
    my_index = lax.axis_index("dp")
    block_ids = jnp.arange(count, dtype=jnp.int32)
    same_owner = owner[:, None] == owner[None, :]
    earlier = block_ids[None, :] < block_ids[:, None]
    rank_within = jnp.sum((same_owner & earlier).astype(jnp.int32), axis=1)
    slot_of = owner * slots + rank_within
    slot_ids = jnp.arange(total_slots, dtype=jnp.int32)
    slot_hits = slot_of[None, :] == slot_ids[:, None]
    filled = jnp.any(slot_hits, axis=1)
    slot_block = jnp.sum(jnp.where(slot_hits, block_ids[None, :], 0), axis=1)
    n_bits = n_data.bit_length() - 1
    if n_bits == 6:
        scatter_orders = [[0, 1, 3, 2, 4, 5], [0, 3, 1, 4, 2, 5]]
        gather_orders = [[5, 4, 2, 3, 1, 0], [2, 5, 4, 1, 3, 0]]
    else:
        scatter_orders = [list(range(n_bits)), list(range(n_bits))]
        gather_orders = [list(range(n_bits))[::-1], list(range(n_bits))[::-1]]
    owned_grad = owner_scatter(local_grad, slot_block, "dp", scatter_orders)
    my_blocks = lax.dynamic_slice_in_dim(slot_block, my_index * slots, slots)
    my_filled = lax.dynamic_slice_in_dim(filled, my_index * slots, slots)
    my_matrix = matrix_index(my_blocks)
    old_each = jnp.take(basis_old, my_matrix, axis=0)
    crossed = butterfly_sum(
        jnp.einsum("scd,sdr->scr", owned_grad, old_each, precision=HIGH), "sub"
    )
    refresh_term = jnp.einsum("scd,scr->sdr", owned_grad, crossed, precision=HIGH)
    matrix_hits = (
        (my_matrix[:, None] == jnp.arange(NMAT, dtype=jnp.int32)[None, :]) & my_filled[:, None]
    ).astype(jnp.float32)
    local_refresh = jnp.einsum("sm,sdr->mdr", matrix_hits, refresh_term, precision=HIGH)
    link_order = [0, 1, 3, 2, 4, 5] if n_bits == 6 else list(range(n_bits))
    flat_refresh = local_refresh.reshape(-1, local_refresh.shape[-1])
    refresh = doubling_merge(
        halving_sum(flat_refresh, "dp", link_order), "dp", link_order[::-1]
    ).reshape(local_refresh.shape)
    refresh_each = jnp.take(refresh, my_matrix, axis=0)
    n_mat, rows, rank = refresh.shape
    gram_part = jnp.einsum("mdr,mds->mrs", refresh, refresh, precision=HIGH)
    cross_part = jnp.einsum("scd,sdr->scr", owned_grad, refresh_each, precision=HIGH)
    gram = rounded_butterfly_sum(gram_part, "sub")
    cross = butterfly_sum(cross_part, "sub")
    norm_sq = jnp.trace(gram, axis1=1, axis2=2) + NORM_EPS
    g0 = gram / norm_sq[:, None, None]
    eye = jnp.broadcast_to(jnp.eye(rank, dtype=jnp.float32), g0.shape)
    poly = 1.5 * eye - 0.5 * g0
    for sweep in range(1, NS_ITERS):
        inner = jnp.einsum("mst,mtu->msu", g0, poly, precision=HIGH)
        h = jnp.einsum("msr,msu->mru", poly, inner, precision=HIGH)
        poly = 1.5 * poly - 0.5 * jnp.einsum("mrs,msu->mru", poly, h, precision=HIGH)
    inv_norm = 1.0 / jnp.sqrt(norm_sq)
    basis = jnp.einsum("mdr,mrs->mds", refresh, poly, precision=HIGH) * inv_norm[:, None, None]
    new_each = jnp.take(basis, my_matrix, axis=0)
    poly_each = jnp.take(poly, my_matrix, axis=0)
    projected_all = jnp.einsum("scr,sru->scu", cross, poly_each, precision=HIGH) * jnp.take(
        inv_norm, my_matrix
    )[:, None, None]
    rows_here = moment1.shape[1]
    projected = lax.dynamic_slice_in_dim(
        projected_all, lax.axis_index("sub") * rows_here, rows_here, axis=1
    )
    first_new = BETA_ONE * moment1 + (1.0 - BETA_ONE) * projected
    second_new = BETA_TWO * moment2 + (1.0 - BETA_TWO) * projected * projected
    adam_step = first_new / CORR_ONE / (jnp.sqrt(second_new / CORR_TWO) + TINY)
    full_step = lax.all_gather(adam_step.astype(jnp.bfloat16), "sub", axis=1, tiled=True).astype(
        adam_step.dtype
    )
    update = jnp.einsum("scr,sdr->scd", full_step, new_each, precision=HIGH)
    new_master = (master.astype(jnp.float32) - LEARN * update).astype(jnp.bfloat16)
    apart = my_index ^ owner
    share = new_master.shape[-1] // len(gather_orders)
    weight_parts = []
    for k, order in enumerate(gather_orders):
        every_slot = doubling_gather(new_master[..., k * share : (k + 1) * share], "dp", order)
        place = sum(((apart >> bit) & 1) << step for step, bit in enumerate(order))
        weight_parts.append(jnp.take(every_slot, place * slots + rank_within, axis=0))
    weights = jnp.concatenate(weight_parts, axis=-1)
    moment1_new = jnp.where(my_filled[:, None, None], first_new, 0.0)
    moment2_new = jnp.where(my_filled[:, None, None], second_new, 0.0)
    return (weights, basis, moment1_new, moment2_new)


def solution(mesh):
    return jax.shard_map(
        local,
        mesh=mesh,
        in_specs=(
            P("dp", None, None, "sub"),
            P(),
            P(None, "sub", None),
            P("dp", "sub", None),
            P("dp", "sub", None),
            P("dp", None, "sub"),
        ),
        out_specs=(
            P(None, None, "sub"),
            P(None, "sub", None),
            P("dp", "sub", None),
            P("dp", "sub", None),
        ),
        check_vma=False,
    )
```

```python
import jax
import jax.numpy as jnp
from jax import lax
from jax.sharding import PartitionSpec as P

D = 1024
VW = 2048
BW = 64
NS_ITERS = 5
NMAT = 4


HIGH = lax.Precision.HIGHEST
SMALL = lax.Precision.HIGH
BETA_ONE = 0.9
BETA_TWO = 0.999
CORR_ONE = 1.0 - 0.9**10
CORR_TWO = 1.0 - 0.999**10
LEARN = 0.05
TINY = 1e-08
NORM_EPS = 1e-06


def matrix_index(block_ids):
    q_blocks = D // BW
    v_blocks = VW // BW
    first = (block_ids >= q_blocks).astype(jnp.int32)
    second = (block_ids >= 2 * q_blocks).astype(jnp.int32)
    third = (block_ids >= 2 * q_blocks + v_blocks).astype(jnp.int32)
    return first + second + third


def butterfly_sum(x, axis):
    size = lax.axis_size(axis)
    for bit in range(size.bit_length() - 1):
        pairs = [(i, i ^ (1 << bit)) for i in range(size)]
        x = x + lax.ppermute(x, axis, pairs)
    return x


def doubling_gather(x, axis, bits):
    size = lax.axis_size(axis)
    for bit in bits:
        pairs = [(i, i ^ (1 << bit)) for i in range(size)]
        x = jnp.concatenate([x, lax.ppermute(x, axis, pairs)], axis=0)
    return x


def halving_sum(x, axis, bits):
    index = lax.axis_index(axis)
    size = lax.axis_size(axis)
    for bit in bits:
        half = x.shape[0] // 2
        upper = ((index >> bit) & 1) == 1
        keep = jnp.where(upper, x[half:], x[:half])
        send = jnp.where(upper, x[:half], x[half:])
        pairs = [(i, i ^ (1 << bit)) for i in range(size)]
        x = keep + lax.ppermute(send, axis, pairs)
    return x


def doubling_merge(x, axis, bits):
    index = lax.axis_index(axis)
    size = lax.axis_size(axis)
    for bit in bits:
        upper = ((index >> bit) & 1) == 1
        pairs = [(i, i ^ (1 << bit)) for i in range(size)]
        got = lax.ppermute(x, axis, pairs)
        x = jnp.where(upper, jnp.concatenate([got, x], axis=0), jnp.concatenate([x, got], axis=0))
    return x


def rounded_butterfly_sum(x, axis):
    size = lax.axis_size(axis)
    for bit in range(size.bit_length() - 1):
        pairs = [(i, i ^ (1 << bit)) for i in range(size)]
        narrow = x.astype(jnp.bfloat16)
        x = narrow.astype(jnp.float32) + lax.ppermute(narrow, axis, pairs).astype(jnp.float32)
    return x


def owner_scatter(local_grad, slot_block, axis, orders):
    index = lax.axis_index(axis)
    size = lax.axis_size(axis)
    slots = slot_block.shape[0] // size
    part = local_grad.shape[1] // len(orders)
    position = jnp.arange(size, dtype=jnp.int32)
    pieces = []
    for k, order in enumerate(orders):
        steps = len(order)
        mask = sum(((position >> (steps - 1 - j)) & 1) << bit for j, bit in enumerate(order))
        dest = index ^ mask
        slot_index = (dest[:, None] * slots + jnp.arange(slots, dtype=jnp.int32)[None, :]).reshape(-1)
        rows = local_grad[:, k * part : (k + 1) * part]
        source = jnp.take(slot_block, slot_index, mode="clip")
        pieces.append(jnp.take(rows, source, axis=0, mode="clip"))
    for j in range(len(orders[0])):
        for k, order in enumerate(orders):
            x = pieces[k]
            half = x.shape[0] // 2
            pairs = [(i, i ^ (1 << order[j])) for i in range(size)]
            pieces[k] = x[:half] + lax.ppermute(x[half:], axis, pairs)
    return jnp.concatenate(pieces, axis=1)


def row_gather(x, axis):
    index = lax.axis_index(axis)
    size = lax.axis_size(axis)
    for bit in range(size.bit_length() - 1):
        upper = ((index >> bit) & 1) == 1
        pairs = [(i, i ^ (1 << bit)) for i in range(size)]
        got = lax.ppermute(x, axis, pairs)
        x = jnp.where(upper, jnp.concatenate([got, x], axis=1), jnp.concatenate([x, got], axis=1))
    return x


def local(partials, owner, basis_old, moment1, moment2, master):
    local_grad = partials[0]
    count = local_grad.shape[0]
    n_data = lax.axis_size("dp")
    slots = moment1.shape[0]
    total_slots = n_data * slots
    my_index = lax.axis_index("dp")
    block_ids = jnp.arange(count, dtype=jnp.int32)
    same_owner = owner[:, None] == owner[None, :]
    earlier = block_ids[None, :] < block_ids[:, None]
    rank_within = jnp.sum((same_owner & earlier).astype(jnp.int32), axis=1)
    slot_of = owner * slots + rank_within
    slot_ids = jnp.arange(total_slots, dtype=jnp.int32)
    slot_hits = slot_of[None, :] == slot_ids[:, None]
    filled = jnp.any(slot_hits, axis=1)
    slot_block = jnp.sum(jnp.where(slot_hits, block_ids[None, :], 0), axis=1)
    n_bits = n_data.bit_length() - 1
    if n_bits == 6:
        scatter_orders = [[0, 1, 3, 2, 4, 5], [0, 3, 1, 4, 2, 5]]
        gather_orders = [[5, 4, 2, 3, 1, 0], [2, 5, 4, 1, 3, 0]]
    else:
        scatter_orders = [list(range(n_bits)), list(range(n_bits))]
        gather_orders = [list(range(n_bits))[::-1], list(range(n_bits))[::-1]]
    owned_grad = owner_scatter(local_grad, slot_block, "dp", scatter_orders)
    my_blocks = lax.dynamic_slice_in_dim(slot_block, my_index * slots, slots)
    my_filled = lax.dynamic_slice_in_dim(filled, my_index * slots, slots)
    my_matrix = matrix_index(my_blocks)
    old_each = jnp.take(basis_old, my_matrix, axis=0, mode="clip")
    crossed = butterfly_sum(
        jnp.einsum("scd,sdr->scr", owned_grad, old_each, precision=HIGH), "sub"
    )
    refresh_term = jnp.einsum("scd,scr->sdr", owned_grad, crossed, precision=HIGH)
    matrix_hits = (
        (my_matrix[:, None] == jnp.arange(NMAT, dtype=jnp.int32)[None, :]) & my_filled[:, None]
    ).astype(jnp.float32)
    local_refresh = jnp.einsum("sm,sdr->mdr", matrix_hits, refresh_term, precision=HIGH)
    link_order = [0, 1, 3, 2, 4, 5] if n_bits == 6 else list(range(n_bits))
    flat_refresh = local_refresh.reshape(-1, local_refresh.shape[-1])
    refresh = doubling_merge(
        halving_sum(flat_refresh, "dp", link_order), "dp", link_order[::-1]
    ).reshape(local_refresh.shape)
    refresh_each = jnp.take(refresh, my_matrix, axis=0, mode="clip")
    n_mat, rows, rank = refresh.shape
    gram_part = jnp.einsum("mdr,mds->mrs", refresh, refresh, precision=HIGH)
    cross_part = jnp.einsum("scd,sdr->scr", owned_grad, refresh_each, precision=HIGH)
    gram = rounded_butterfly_sum(gram_part, "sub")
    cross = butterfly_sum(cross_part, "sub")
    norm_sq = jnp.trace(gram, axis1=1, axis2=2) + NORM_EPS
    g0 = gram / norm_sq[:, None, None]
    eye = jnp.broadcast_to(jnp.eye(rank, dtype=jnp.float32), g0.shape)
    poly = 1.5 * eye - 0.5 * g0
    for sweep in range(1, NS_ITERS):
        inner = jnp.einsum("mst,mtu->msu", g0, poly, precision=SMALL)
        h = jnp.einsum("msr,msu->mru", poly, inner, precision=SMALL)
        poly = 1.5 * poly - 0.5 * jnp.einsum("mrs,msu->mru", poly, h, precision=SMALL)
    inv_norm = 1.0 / jnp.sqrt(norm_sq)
    basis = jnp.einsum("mdr,mrs->mds", refresh, poly, precision=HIGH) * inv_norm[:, None, None]
    new_each = jnp.take(basis, my_matrix, axis=0, mode="clip")
    poly_each = jnp.take(poly, my_matrix, axis=0, mode="clip")
    projected_all = jnp.einsum("scr,sru->scu", cross, poly_each, precision=HIGH) * jnp.take(
        inv_norm, my_matrix
    )[:, None, None]
    rows_here = moment1.shape[1]
    projected = lax.dynamic_slice_in_dim(
        projected_all, lax.axis_index("sub") * rows_here, rows_here, axis=1
    )
    first_new = BETA_ONE * moment1 + (1.0 - BETA_ONE) * projected
    second_new = BETA_TWO * moment2 + (1.0 - BETA_TWO) * projected * projected
    adam_step = first_new / CORR_ONE / (jnp.sqrt(second_new / CORR_TWO) + TINY)
    full_step = row_gather(adam_step.astype(jnp.bfloat16), "sub").astype(adam_step.dtype)
    update = jnp.einsum("scr,sdr->scd", full_step, new_each, precision=HIGH)
    new_master = (master.astype(jnp.float32) - LEARN * update).astype(jnp.bfloat16)
    apart = my_index ^ owner
    share = new_master.shape[1] // len(gather_orders)
    weight_parts = []
    for k, order in enumerate(gather_orders):
        every_slot = doubling_gather(new_master[:, k * share : (k + 1) * share], "dp", order)
        place = sum(((apart >> bit) & 1) << step for step, bit in enumerate(order))
        weight_parts.append(
            jnp.take(every_slot, place * slots + rank_within, axis=0, mode="clip")
        )
    weights = jnp.concatenate(weight_parts, axis=1)
    moment1_new = jnp.where(my_filled[:, None, None], first_new, 0.0)
    moment2_new = jnp.where(my_filled[:, None, None], second_new, 0.0)
    return (weights, basis, moment1_new, moment2_new)


def solution(mesh):
    return jax.shard_map(
        local,
        mesh=mesh,
        in_specs=(
            P("dp", None, None, "sub"),
            P(),
            P(None, "sub", None),
            P("dp", "sub", None),
            P("dp", "sub", None),
            P("dp", None, "sub"),
        ),
        out_specs=(
            P(None, None, "sub"),
            P(None, "sub", None),
            P("dp", "sub", None),
            P("dp", "sub", None),
        ),
        check_vma=False,
    )
```

```python
import jax
import jax.numpy as jnp
from jax import lax
from jax.sharding import PartitionSpec as P

D = 1024
VW = 2048
BW = 64
NS_ITERS = 5
NMAT = 4


HIGH = lax.Precision.HIGHEST
SMALL = lax.Precision.HIGH
BETA_ONE = 0.9
BETA_TWO = 0.999
CORR_ONE = 1.0 - 0.9**10
CORR_TWO = 1.0 - 0.999**10
LEARN = 0.05
TINY = 1e-08
NORM_EPS = 1e-06


def matrix_index(block_ids):
    q_blocks = D // BW
    v_blocks = VW // BW
    first = (block_ids >= q_blocks).astype(jnp.int32)
    second = (block_ids >= 2 * q_blocks).astype(jnp.int32)
    third = (block_ids >= 2 * q_blocks + v_blocks).astype(jnp.int32)
    return first + second + third


def butterfly_sum(x, axis):
    size = lax.axis_size(axis)
    for bit in range(size.bit_length() - 1):
        pairs = [(i, i ^ (1 << bit)) for i in range(size)]
        x = x + lax.ppermute(x, axis, pairs)
    return x


def doubling_gather(x, axis, bits):
    size = lax.axis_size(axis)
    for bit in bits:
        pairs = [(i, i ^ (1 << bit)) for i in range(size)]
        x = jnp.concatenate([x, lax.ppermute(x, axis, pairs)], axis=0)
    return x


def halving_sum(x, axis, bits):
    index = lax.axis_index(axis)
    size = lax.axis_size(axis)
    for bit in bits:
        half = x.shape[0] // 2
        upper = ((index >> bit) & 1) == 1
        keep = jnp.where(upper, x[half:], x[:half])
        send = jnp.where(upper, x[:half], x[half:])
        pairs = [(i, i ^ (1 << bit)) for i in range(size)]
        x = keep + lax.ppermute(send, axis, pairs)
    return x


def doubling_merge(x, axis, bits):
    index = lax.axis_index(axis)
    size = lax.axis_size(axis)
    for bit in bits:
        upper = ((index >> bit) & 1) == 1
        pairs = [(i, i ^ (1 << bit)) for i in range(size)]
        got = lax.ppermute(x, axis, pairs)
        x = jnp.where(upper, jnp.concatenate([got, x], axis=0), jnp.concatenate([x, got], axis=0))
    return x


def rounded_butterfly_sum(x, axis, bits):
    size = lax.axis_size(axis)
    for bit in bits:
        pairs = [(i, i ^ (1 << bit)) for i in range(size)]
        narrow = x.astype(jnp.bfloat16)
        x = narrow.astype(jnp.float32) + lax.ppermute(narrow, axis, pairs).astype(jnp.float32)
    return x


def owner_scatter(local_grad, slot_block, axis, orders):
    index = lax.axis_index(axis)
    size = lax.axis_size(axis)
    slots = slot_block.shape[0] // size
    count, rows, cols = local_grad.shape
    n_pieces = len(orders)
    part = rows // n_pieces
    flat = local_grad.reshape(count * n_pieces, part, cols)
    position = jnp.arange(size, dtype=jnp.int32)
    halves = []
    for k, order in enumerate(orders):
        steps = len(order)
        mask = sum(((position >> (steps - 1 - j)) & 1) << bit for j, bit in enumerate(order))
        dest = index ^ mask
        slot_index = (dest[:, None] * slots + jnp.arange(slots, dtype=jnp.int32)[None, :]).reshape(-1)
        source = jnp.take(slot_block, slot_index, mode="clip") * n_pieces + k
        middle = source.shape[0] // 2
        halves.append(
            (
                jnp.take(flat, source[:middle], axis=0, mode="clip"),
                jnp.take(flat, source[middle:], axis=0, mode="clip"),
            )
        )
    pieces = [None] * n_pieces
    for j in range(len(orders[0])):
        for k, order in enumerate(orders):
            if j == 0:
                keep, send = halves[k]
            else:
                x = pieces[k]
                middle = x.shape[0] // 2
                keep, send = x[:middle], x[middle:]
            pairs = [(i, i ^ (1 << order[j])) for i in range(size)]
            pieces[k] = keep + lax.ppermute(send, axis, pairs)
    return jnp.concatenate(pieces, axis=1)


def row_gather(x, axis):
    index = lax.axis_index(axis)
    size = lax.axis_size(axis)
    for bit in range(size.bit_length() - 1):
        upper = ((index >> bit) & 1) == 1
        pairs = [(i, i ^ (1 << bit)) for i in range(size)]
        got = lax.ppermute(x, axis, pairs)
        x = jnp.where(upper, jnp.concatenate([got, x], axis=1), jnp.concatenate([x, got], axis=1))
    return x


def local(partials, owner, basis_old, moment1, moment2, master):
    local_grad = partials[0]
    count = local_grad.shape[0]
    n_data = lax.axis_size("dp")
    slots = moment1.shape[0]
    total_slots = n_data * slots
    my_index = lax.axis_index("dp")
    block_ids = jnp.arange(count, dtype=jnp.int32)
    same_owner = owner[:, None] == owner[None, :]
    earlier = block_ids[None, :] < block_ids[:, None]
    rank_within = jnp.sum((same_owner & earlier).astype(jnp.int32), axis=1)
    slot_of = owner * slots + rank_within
    slot_ids = jnp.arange(total_slots, dtype=jnp.int32)
    slot_hits = slot_of[None, :] == slot_ids[:, None]
    filled = jnp.any(slot_hits, axis=1)
    slot_block = jnp.sum(jnp.where(slot_hits, block_ids[None, :], 0), axis=1)
    n_bits = n_data.bit_length() - 1
    if n_bits == 6:
        scatter_orders = [[0, 1, 3, 2, 4, 5], [0, 3, 1, 4, 2, 5]]
        gather_orders = [[5, 4, 2, 3, 1, 0], [2, 5, 4, 1, 3, 0]]
    else:
        scatter_orders = [list(range(n_bits)), list(range(n_bits))]
        gather_orders = [list(range(n_bits))[::-1], list(range(n_bits))[::-1]]
    owned_grad = owner_scatter(local_grad, slot_block, "dp", scatter_orders)
    my_blocks = lax.dynamic_slice_in_dim(slot_block, my_index * slots, slots)
    my_filled = lax.dynamic_slice_in_dim(filled, my_index * slots, slots)
    my_matrix = matrix_index(my_blocks)
    old_each = jnp.take(basis_old, my_matrix, axis=0, mode="clip")
    crossed = butterfly_sum(
        jnp.einsum("scd,sdr->scr", owned_grad, old_each, precision=HIGH), "sub"
    )
    refresh_term = jnp.einsum("scd,scr->sdr", owned_grad, crossed, precision=HIGH)
    matrix_hits = (
        (my_matrix[:, None] == jnp.arange(NMAT, dtype=jnp.int32)[None, :]) & my_filled[:, None]
    ).astype(jnp.float32)
    local_refresh = jnp.einsum("sm,sdr->mdr", matrix_hits, refresh_term, precision=HIGH)
    link_order = [0, 1, 3, 2, 4, 5] if n_bits == 6 else list(range(n_bits))
    flat_refresh = local_refresh.reshape(-1, local_refresh.shape[-1])
    refresh = doubling_merge(
        halving_sum(flat_refresh, "dp", link_order), "dp", link_order[::-1]
    ).reshape(local_refresh.shape)
    refresh_each = jnp.take(refresh, my_matrix, axis=0, mode="clip")
    n_mat, rows, rank = refresh.shape
    gram_part = jnp.einsum("mdr,mds->mrs", refresh, refresh, precision=HIGH)
    cross_part = jnp.einsum("scd,sdr->scr", owned_grad, refresh_each, precision=HIGH)
    sub_bits = list(range(lax.axis_size("sub").bit_length() - 1))
    split = n_mat // 2
    gram = jnp.concatenate(
        [
            rounded_butterfly_sum(gram_part[:split], "sub", sub_bits),
            rounded_butterfly_sum(gram_part[split:], "sub", sub_bits[::-1]),
        ],
        axis=0,
    )
    cross = butterfly_sum(cross_part, "sub")
    norm_sq = jnp.trace(gram, axis1=1, axis2=2) + NORM_EPS
    g0 = gram / norm_sq[:, None, None]
    eye = jnp.broadcast_to(jnp.eye(rank, dtype=jnp.float32), g0.shape)
    poly = 1.5 * eye - 0.5 * g0
    for sweep in range(1, NS_ITERS):
        inner = jnp.einsum("mst,mtu->msu", g0, poly, precision=SMALL)
        h = jnp.einsum("msr,msu->mru", poly, inner, precision=SMALL)
        poly = 1.5 * poly - 0.5 * jnp.einsum("mrs,msu->mru", poly, h, precision=SMALL)
    inv_norm = 1.0 / jnp.sqrt(norm_sq)
    basis = jnp.einsum("mdr,mrs->mds", refresh, poly, precision=HIGH) * inv_norm[:, None, None]
    new_each = jnp.take(basis, my_matrix, axis=0, mode="clip")
    poly_each = jnp.take(poly, my_matrix, axis=0, mode="clip")
    projected_all = jnp.einsum("scr,sru->scu", cross, poly_each, precision=HIGH) * jnp.take(
        inv_norm, my_matrix
    )[:, None, None]
    rows_here = moment1.shape[1]
    projected = lax.dynamic_slice_in_dim(
        projected_all, lax.axis_index("sub") * rows_here, rows_here, axis=1
    )
    first_new = BETA_ONE * moment1 + (1.0 - BETA_ONE) * projected
    second_new = BETA_TWO * moment2 + (1.0 - BETA_TWO) * projected * projected
    adam_step = first_new / CORR_ONE / (jnp.sqrt(second_new / CORR_TWO) + TINY)
    full_step = row_gather(adam_step.astype(jnp.bfloat16), "sub").astype(adam_step.dtype)
    update = jnp.einsum("scr,sdr->scd", full_step, new_each, precision=HIGH)
    new_master = (master.astype(jnp.float32) - LEARN * update).astype(jnp.bfloat16)
    apart = my_index ^ owner
    share = new_master.shape[1] // len(gather_orders)
    weight_parts = []
    for k, order in enumerate(gather_orders):
        every_slot = doubling_gather(new_master[:, k * share : (k + 1) * share], "dp", order)
        place = sum(((apart >> bit) & 1) << step for step, bit in enumerate(order))
        weight_parts.append(
            jnp.take(every_slot, place * slots + rank_within, axis=0, mode="clip")
        )
    weights = jnp.concatenate(weight_parts, axis=1)
    moment1_new = jnp.where(my_filled[:, None, None], first_new, 0.0)
    moment2_new = jnp.where(my_filled[:, None, None], second_new, 0.0)
    return (weights, basis, moment1_new, moment2_new)


def solution(mesh):
    return jax.shard_map(
        local,
        mesh=mesh,
        in_specs=(
            P("dp", None, None, "sub"),
            P(),
            P(None, "sub", None),
            P("dp", "sub", None),
            P("dp", "sub", None),
            P("dp", None, "sub"),
        ),
        out_specs=(
            P(None, None, "sub"),
            P(None, "sub", None),
            P("dp", "sub", None),
            P("dp", "sub", None),
        ),
        check_vma=False,
    )
```

```python
import jax
import jax.numpy as jnp
from jax import lax
from jax.sharding import PartitionSpec as P

D = 1024
VW = 2048
BW = 64
NS_ITERS = 5
NMAT = 4


HIGH = lax.Precision.HIGH
SMALL = lax.Precision.HIGH
BETA_ONE = 0.9
BETA_TWO = 0.999
CORR_ONE = 1.0 - 0.9**10
CORR_TWO = 1.0 - 0.999**10
LEARN = 0.05
TINY = 1e-08
NORM_EPS = 1e-06


def matrix_index(block_ids):
    q_blocks = D // BW
    v_blocks = VW // BW
    first = (block_ids >= q_blocks).astype(jnp.int32)
    second = (block_ids >= 2 * q_blocks).astype(jnp.int32)
    third = (block_ids >= 2 * q_blocks + v_blocks).astype(jnp.int32)
    return first + second + third


def butterfly_sum(x, axis):
    size = lax.axis_size(axis)
    for bit in range(size.bit_length() - 1):
        pairs = [(i, i ^ (1 << bit)) for i in range(size)]
        x = x + lax.ppermute(x, axis, pairs)
    return x


def doubling_gather(x, axis, bits):
    size = lax.axis_size(axis)
    for bit in bits:
        pairs = [(i, i ^ (1 << bit)) for i in range(size)]
        x = jnp.concatenate([x, lax.ppermute(x, axis, pairs)], axis=0)
    return x


def halving_sum(x, axis, bits):
    index = lax.axis_index(axis)
    size = lax.axis_size(axis)
    for bit in bits:
        half = x.shape[0] // 2
        upper = ((index >> bit) & 1) == 1
        keep = jnp.where(upper, x[half:], x[:half])
        send = jnp.where(upper, x[:half], x[half:])
        pairs = [(i, i ^ (1 << bit)) for i in range(size)]
        x = keep + lax.ppermute(send, axis, pairs)
    return x


def doubling_merge(x, axis, bits):
    index = lax.axis_index(axis)
    size = lax.axis_size(axis)
    for bit in bits:
        upper = ((index >> bit) & 1) == 1
        pairs = [(i, i ^ (1 << bit)) for i in range(size)]
        got = lax.ppermute(x, axis, pairs)
        x = jnp.where(upper, jnp.concatenate([got, x], axis=0), jnp.concatenate([x, got], axis=0))
    return x


def rounded_butterfly_sum(x, axis, bits):
    size = lax.axis_size(axis)
    for bit in bits:
        pairs = [(i, i ^ (1 << bit)) for i in range(size)]
        narrow = x.astype(jnp.bfloat16)
        x = narrow.astype(jnp.float32) + lax.ppermute(narrow, axis, pairs).astype(jnp.float32)
    return x


def owner_scatter(local_grad, slot_block, axis, orders):
    index = lax.axis_index(axis)
    size = lax.axis_size(axis)
    slots = slot_block.shape[0] // size
    count, rows, cols = local_grad.shape
    n_pieces = len(orders)
    part = rows // n_pieces
    flat = local_grad.reshape(count * n_pieces, part, cols)
    position = jnp.arange(size, dtype=jnp.int32)
    halves = []
    for k, order in enumerate(orders):
        steps = len(order)
        mask = sum(((position >> (steps - 1 - j)) & 1) << bit for j, bit in enumerate(order))
        dest = index ^ mask
        slot_index = (dest[:, None] * slots + jnp.arange(slots, dtype=jnp.int32)[None, :]).reshape(-1)
        source = jnp.take(slot_block, slot_index, mode="clip") * n_pieces + k
        middle = source.shape[0] // 2
        halves.append(
            (
                jnp.take(flat, source[:middle], axis=0, mode="clip"),
                jnp.take(flat, source[middle:], axis=0, mode="clip"),
            )
        )
    pieces = [None] * n_pieces
    for j in range(len(orders[0])):
        for k, order in enumerate(orders):
            if j == 0:
                keep, send = halves[k]
            else:
                x = pieces[k]
                middle = x.shape[0] // 2
                keep, send = x[:middle], x[middle:]
            pairs = [(i, i ^ (1 << order[j])) for i in range(size)]
            pieces[k] = keep + lax.ppermute(send, axis, pairs)
    return jnp.concatenate(pieces, axis=1)


def row_gather(x, axis):
    index = lax.axis_index(axis)
    size = lax.axis_size(axis)
    for bit in range(size.bit_length() - 1):
        upper = ((index >> bit) & 1) == 1
        pairs = [(i, i ^ (1 << bit)) for i in range(size)]
        got = lax.ppermute(x, axis, pairs)
        x = jnp.where(upper, jnp.concatenate([got, x], axis=1), jnp.concatenate([x, got], axis=1))
    return x


def local(partials, owner, basis_old, moment1, moment2, master):
    local_grad = partials[0]
    count = local_grad.shape[0]
    n_data = lax.axis_size("dp")
    slots = moment1.shape[0]
    total_slots = n_data * slots
    my_index = lax.axis_index("dp")
    block_ids = jnp.arange(count, dtype=jnp.int32)
    same_owner = owner[:, None] == owner[None, :]
    earlier = block_ids[None, :] < block_ids[:, None]
    rank_within = jnp.sum((same_owner & earlier).astype(jnp.int32), axis=1)
    slot_of = owner * slots + rank_within
    slot_ids = jnp.arange(total_slots, dtype=jnp.int32)
    slot_hits = slot_of[None, :] == slot_ids[:, None]
    filled = jnp.any(slot_hits, axis=1)
    slot_block = jnp.sum(jnp.where(slot_hits, block_ids[None, :], 0), axis=1)
    n_bits = n_data.bit_length() - 1
    if n_bits == 6:
        scatter_orders = [[0, 1, 3, 2, 4, 5], [0, 3, 1, 4, 2, 5]]
        gather_orders = [[5, 4, 2, 3, 1, 0], [2, 5, 4, 1, 3, 0]]
    else:
        scatter_orders = [list(range(n_bits)), list(range(n_bits))]
        gather_orders = [list(range(n_bits))[::-1], list(range(n_bits))[::-1]]
    owned_grad = owner_scatter(local_grad, slot_block, "dp", scatter_orders)
    my_blocks = lax.dynamic_slice_in_dim(slot_block, my_index * slots, slots)
    my_filled = lax.dynamic_slice_in_dim(filled, my_index * slots, slots)
    my_matrix = matrix_index(my_blocks)
    old_each = jnp.take(basis_old, my_matrix, axis=0, mode="clip")
    crossed = butterfly_sum(
        jnp.einsum("scd,sdr->scr", owned_grad, old_each, precision=HIGH), "sub"
    )
    refresh_term = jnp.einsum("scd,scr->sdr", owned_grad, crossed, precision=HIGH)
    matrix_hits = (
        (my_matrix[:, None] == jnp.arange(NMAT, dtype=jnp.int32)[None, :]) & my_filled[:, None]
    ).astype(jnp.float32)
    local_refresh = jnp.einsum("sm,sdr->mdr", matrix_hits, refresh_term, precision=HIGH)
    link_order = [0, 1, 3, 2, 4, 5] if n_bits == 6 else list(range(n_bits))
    flat_refresh = local_refresh.reshape(-1, local_refresh.shape[-1])
    refresh = doubling_merge(
        halving_sum(flat_refresh, "dp", link_order), "dp", link_order[::-1]
    ).reshape(local_refresh.shape)
    refresh_each = jnp.take(refresh, my_matrix, axis=0, mode="clip")
    n_mat, rows, rank = refresh.shape
    gram_part = jnp.einsum("mdr,mds->mrs", refresh, refresh, precision=HIGH)
    cross_part = jnp.einsum("scd,sdr->scr", owned_grad, refresh_each, precision=HIGH)
    sub_bits = list(range(lax.axis_size("sub").bit_length() - 1))
    split = n_mat // 2
    gram = jnp.concatenate(
        [
            rounded_butterfly_sum(gram_part[:split], "sub", sub_bits),
            rounded_butterfly_sum(gram_part[split:], "sub", sub_bits[::-1]),
        ],
        axis=0,
    )
    cross = butterfly_sum(cross_part, "sub")
    norm_sq = jnp.trace(gram, axis1=1, axis2=2) + NORM_EPS
    g0 = gram / norm_sq[:, None, None]
    eye = jnp.broadcast_to(jnp.eye(rank, dtype=jnp.float32), g0.shape)
    poly = 1.5 * eye - 0.5 * g0
    for sweep in range(1, NS_ITERS):
        inner = jnp.einsum("mst,mtu->msu", g0, poly, precision=SMALL)
        h = jnp.einsum("msr,msu->mru", poly, inner, precision=SMALL)
        poly = 1.5 * poly - 0.5 * jnp.einsum("mrs,msu->mru", poly, h, precision=SMALL)
    inv_norm = 1.0 / jnp.sqrt(norm_sq)
    basis = jnp.einsum("mdr,mrs->mds", refresh, poly, precision=HIGH) * inv_norm[:, None, None]
    new_each = jnp.take(basis, my_matrix, axis=0, mode="clip")
    poly_each = jnp.take(poly, my_matrix, axis=0, mode="clip")
    projected_all = jnp.einsum("scr,sru->scu", cross, poly_each, precision=HIGH) * jnp.take(
        inv_norm, my_matrix
    )[:, None, None]
    rows_here = moment1.shape[1]
    projected = lax.dynamic_slice_in_dim(
        projected_all, lax.axis_index("sub") * rows_here, rows_here, axis=1
    )
    first_new = BETA_ONE * moment1 + (1.0 - BETA_ONE) * projected
    second_new = BETA_TWO * moment2 + (1.0 - BETA_TWO) * projected * projected
    adam_step = first_new / CORR_ONE / (jnp.sqrt(second_new / CORR_TWO) + TINY)
    full_step = row_gather(adam_step.astype(jnp.bfloat16), "sub").astype(adam_step.dtype)
    update = jnp.einsum("scr,sdr->scd", full_step, new_each, precision=HIGH)
    new_master = (master.astype(jnp.float32) - LEARN * update).astype(jnp.bfloat16)
    apart = my_index ^ owner
    share = new_master.shape[1] // len(gather_orders)
    weight_parts = []
    for k, order in enumerate(gather_orders):
        every_slot = doubling_gather(new_master[:, k * share : (k + 1) * share], "dp", order)
        place = sum(((apart >> bit) & 1) << step for step, bit in enumerate(order))
        weight_parts.append(
            jnp.take(every_slot, place * slots + rank_within, axis=0, mode="clip")
        )
    weights = jnp.concatenate(weight_parts, axis=1)
    moment1_new = jnp.where(my_filled[:, None, None], first_new, 0.0)
    moment2_new = jnp.where(my_filled[:, None, None], second_new, 0.0)
    return (weights, basis, moment1_new, moment2_new)


def solution(mesh):
    return jax.shard_map(
        local,
        mesh=mesh,
        in_specs=(
            P("dp", None, None, "sub"),
            P(),
            P(None, "sub", None),
            P("dp", "sub", None),
            P("dp", "sub", None),
            P("dp", None, "sub"),
        ),
        out_specs=(
            P(None, None, "sub"),
            P(None, "sub", None),
            P("dp", "sub", None),
            P("dp", "sub", None),
        ),
        check_vma=False,
    )
```

```python
import jax
import jax.numpy as jnp
from jax import lax
from jax.sharding import PartitionSpec as P

D = 1024
VW = 2048
BW = 64
NS_ITERS = 5
NMAT = 4


HIGH = lax.Precision.HIGH
SMALL = lax.Precision.HIGH
BETA_ONE = 0.9
BETA_TWO = 0.999
CORR_ONE = 1.0 - 0.9**10
CORR_TWO = 1.0 - 0.999**10
LEARN = 0.05
TINY = 1e-08
NORM_EPS = 1e-06


def matrix_index(block_ids):
    q_blocks = D // BW
    v_blocks = VW // BW
    first = (block_ids >= q_blocks).astype(jnp.int32)
    second = (block_ids >= 2 * q_blocks).astype(jnp.int32)
    third = (block_ids >= 2 * q_blocks + v_blocks).astype(jnp.int32)
    return first + second + third


def butterfly_sum(x, axis):
    size = lax.axis_size(axis)
    for bit in range(size.bit_length() - 1):
        pairs = [(i, i ^ (1 << bit)) for i in range(size)]
        x = x + lax.ppermute(x, axis, pairs)
    return x


def doubling_gather(x, axis, bits):
    size = lax.axis_size(axis)
    for bit in bits:
        pairs = [(i, i ^ (1 << bit)) for i in range(size)]
        x = jnp.concatenate([x, lax.ppermute(x, axis, pairs)], axis=0)
    return x


def halving_sum(x, axis, bits):
    index = lax.axis_index(axis)
    size = lax.axis_size(axis)
    for bit in bits:
        half = x.shape[0] // 2
        upper = ((index >> bit) & 1) == 1
        keep = jnp.where(upper, x[half:], x[:half])
        send = jnp.where(upper, x[:half], x[half:])
        pairs = [(i, i ^ (1 << bit)) for i in range(size)]
        x = keep + lax.ppermute(send, axis, pairs)
    return x


def doubling_merge(x, axis, bits):
    index = lax.axis_index(axis)
    size = lax.axis_size(axis)
    for bit in bits:
        upper = ((index >> bit) & 1) == 1
        pairs = [(i, i ^ (1 << bit)) for i in range(size)]
        got = lax.ppermute(x, axis, pairs)
        x = jnp.where(upper, jnp.concatenate([got, x], axis=0), jnp.concatenate([x, got], axis=0))
    return x


def rounded_butterfly_sum(x, axis, bits):
    size = lax.axis_size(axis)
    for bit in bits:
        pairs = [(i, i ^ (1 << bit)) for i in range(size)]
        narrow = x.astype(jnp.bfloat16)
        x = narrow.astype(jnp.float32) + lax.ppermute(narrow, axis, pairs).astype(jnp.float32)
    return x


def owner_scatter(local_grad, slot_block, axis, orders):
    index = lax.axis_index(axis)
    size = lax.axis_size(axis)
    slots = slot_block.shape[0] // size
    count, rows, cols = local_grad.shape
    n_pieces = len(orders)
    part = rows // n_pieces
    flat = local_grad.reshape(count * n_pieces, part, cols)
    position = jnp.arange(size, dtype=jnp.int32)
    halves = []
    for k, order in enumerate(orders):
        steps = len(order)
        mask = sum(((position >> (steps - 1 - j)) & 1) << bit for j, bit in enumerate(order))
        dest = index ^ mask
        slot_index = (dest[:, None] * slots + jnp.arange(slots, dtype=jnp.int32)[None, :]).reshape(-1)
        source = jnp.take(slot_block, slot_index, mode="clip") * n_pieces + k
        middle = source.shape[0] // 2
        halves.append(
            (
                jnp.take(flat, source[:middle], axis=0, mode="clip"),
                jnp.take(flat, source[middle:], axis=0, mode="clip"),
            )
        )
    pieces = [None] * n_pieces
    for j in range(len(orders[0])):
        for k, order in enumerate(orders):
            if j == 0:
                keep, send = halves[k]
            else:
                x = pieces[k]
                middle = x.shape[0] // 2
                keep, send = x[:middle], x[middle:]
            pairs = [(i, i ^ (1 << order[j])) for i in range(size)]
            pieces[k] = keep + lax.ppermute(send, axis, pairs)
    return jnp.concatenate(pieces, axis=1)


def row_gather(x, axis):
    index = lax.axis_index(axis)
    size = lax.axis_size(axis)
    for bit in range(size.bit_length() - 1):
        upper = ((index >> bit) & 1) == 1
        pairs = [(i, i ^ (1 << bit)) for i in range(size)]
        got = lax.ppermute(x, axis, pairs)
        x = jnp.where(upper, jnp.concatenate([got, x], axis=1), jnp.concatenate([x, got], axis=1))
    return x


def local(partials, owner, basis_old, moment1, moment2, master):
    local_grad = partials[0]
    count = local_grad.shape[0]
    n_data = lax.axis_size("dp")
    slots = moment1.shape[0]
    total_slots = n_data * slots
    my_index = lax.axis_index("dp")
    block_ids = jnp.arange(count, dtype=jnp.int32)
    same_owner = owner[:, None] == owner[None, :]
    earlier = block_ids[None, :] < block_ids[:, None]
    rank_within = jnp.sum((same_owner & earlier).astype(jnp.int32), axis=1)
    slot_of = owner * slots + rank_within
    slot_ids = jnp.arange(total_slots, dtype=jnp.int32)
    slot_hits = slot_of[None, :] == slot_ids[:, None]
    filled = jnp.any(slot_hits, axis=1)
    slot_block = jnp.sum(jnp.where(slot_hits, block_ids[None, :], 0), axis=1)
    n_bits = n_data.bit_length() - 1
    if n_bits == 6:
        scatter_orders = [[0, 1, 3, 2, 4, 5], [0, 3, 1, 4, 2, 5]]
        gather_orders = [[5, 4, 2, 3, 1, 0], [2, 5, 4, 1, 3, 0]]
    else:
        scatter_orders = [list(range(n_bits)), list(range(n_bits))]
        gather_orders = [list(range(n_bits))[::-1], list(range(n_bits))[::-1]]
    owned_grad = owner_scatter(local_grad, slot_block, "dp", scatter_orders)
    my_blocks = lax.dynamic_slice_in_dim(slot_block, my_index * slots, slots)
    my_filled = lax.dynamic_slice_in_dim(filled, my_index * slots, slots)
    my_matrix = matrix_index(my_blocks)
    old_each = jnp.take(basis_old, my_matrix, axis=0, mode="clip")
    crossed = butterfly_sum(
        jnp.einsum("scd,sdr->scr", owned_grad, old_each, precision=HIGH), "sub"
    )
    refresh_term = jnp.einsum("scd,scr->sdr", owned_grad, crossed, precision=HIGH)
    matrix_hits = (
        (my_matrix[:, None] == jnp.arange(NMAT, dtype=jnp.int32)[None, :]) & my_filled[:, None]
    ).astype(jnp.float32)
    local_refresh = jnp.einsum("sm,sdr->mdr", matrix_hits, refresh_term, precision=HIGH)
    link_order = [0, 1, 3, 2, 4, 5] if n_bits == 6 else list(range(n_bits))
    flat_refresh = local_refresh.reshape(-1, local_refresh.shape[-1])
    refresh = doubling_merge(
        halving_sum(flat_refresh, "dp", link_order), "dp", link_order[::-1]
    ).reshape(local_refresh.shape)
    refresh_each = jnp.take(refresh, my_matrix, axis=0, mode="clip")
    n_mat, rows, rank = refresh.shape
    gram_part = jnp.einsum("mdr,mds->mrs", refresh, refresh, precision=HIGH)
    cross_part = jnp.einsum("scd,sdr->scr", owned_grad, refresh_each, precision=HIGH)
    sub_bits = list(range(lax.axis_size("sub").bit_length() - 1))
    split = n_mat // 2
    gram = jnp.concatenate(
        [
            rounded_butterfly_sum(gram_part[:split], "sub", sub_bits),
            rounded_butterfly_sum(gram_part[split:], "sub", sub_bits[::-1]),
        ],
        axis=0,
    )
    cross = butterfly_sum(cross_part, "sub")
    norm_sq = jnp.trace(gram, axis1=1, axis2=2) + NORM_EPS
    g0 = gram / norm_sq[:, None, None]
    eye = jnp.broadcast_to(jnp.eye(rank, dtype=jnp.float32), g0.shape)
    poly = 1.5 * eye - 0.5 * g0
    def sweep_step(sweep, poly):
        inner = jnp.einsum("mst,mtu->msu", g0, poly, precision=SMALL)
        h = jnp.einsum("msr,msu->mru", poly, inner, precision=SMALL)
        return 1.5 * poly - 0.5 * jnp.einsum("mrs,msu->mru", poly, h, precision=SMALL)

    poly = lax.fori_loop(1, NS_ITERS, sweep_step, poly)
    inv_norm = 1.0 / jnp.sqrt(norm_sq)
    basis = jnp.einsum("mdr,mrs->mds", refresh, poly, precision=HIGH) * inv_norm[:, None, None]
    new_each = jnp.take(basis, my_matrix, axis=0, mode="clip")
    poly_each = jnp.take(poly, my_matrix, axis=0, mode="clip")
    projected_all = jnp.einsum("scr,sru->scu", cross, poly_each, precision=HIGH) * jnp.take(
        inv_norm, my_matrix
    )[:, None, None]
    rows_here = moment1.shape[1]
    projected = lax.dynamic_slice_in_dim(
        projected_all, lax.axis_index("sub") * rows_here, rows_here, axis=1
    )
    first_new = BETA_ONE * moment1 + (1.0 - BETA_ONE) * projected
    second_new = BETA_TWO * moment2 + (1.0 - BETA_TWO) * projected * projected
    adam_step = first_new / CORR_ONE / (jnp.sqrt(second_new / CORR_TWO) + TINY)
    full_step = row_gather(adam_step.astype(jnp.bfloat16), "sub").astype(adam_step.dtype)
    update = jnp.einsum("scr,sdr->scd", full_step, new_each, precision=HIGH)
    new_master = (master.astype(jnp.float32) - LEARN * update).astype(jnp.bfloat16)
    apart = my_index ^ owner
    share = new_master.shape[1] // len(gather_orders)
    weight_parts = []
    for k, order in enumerate(gather_orders):
        every_slot = doubling_gather(new_master[:, k * share : (k + 1) * share], "dp", order)
        place = sum(((apart >> bit) & 1) << step for step, bit in enumerate(order))
        weight_parts.append(
            jnp.take(every_slot, place * slots + rank_within, axis=0, mode="clip")
        )
    weights = jnp.concatenate(weight_parts, axis=1)
    moment1_new = jnp.where(my_filled[:, None, None], first_new, 0.0)
    moment2_new = jnp.where(my_filled[:, None, None], second_new, 0.0)
    return (weights, basis, moment1_new, moment2_new)


def solution(mesh):
    return jax.shard_map(
        local,
        mesh=mesh,
        in_specs=(
            P("dp", None, None, "sub"),
            P(),
            P(None, "sub", None),
            P("dp", "sub", None),
            P("dp", "sub", None),
            P("dp", None, "sub"),
        ),
        out_specs=(
            P(None, None, "sub"),
            P(None, "sub", None),
            P("dp", "sub", None),
            P("dp", "sub", None),
        ),
        check_vma=False,
    )
```

```python
import jax
import jax.numpy as jnp
from jax import lax
from jax.sharding import PartitionSpec as P

D = 1024
VW = 2048
BW = 64
NS_ITERS = 5
NMAT = 4


HIGH = lax.Precision.HIGH
SMALL = lax.Precision.HIGH
BETA_ONE = 0.9
BETA_TWO = 0.999
CORR_ONE = 1.0 - 0.9**10
CORR_TWO = 1.0 - 0.999**10
LEARN = 0.05
TINY = 1e-08
NORM_EPS = 1e-06


def matrix_index(block_ids):
    q_blocks = D // BW
    v_blocks = VW // BW
    first = (block_ids >= q_blocks).astype(jnp.int32)
    second = (block_ids >= 2 * q_blocks).astype(jnp.int32)
    third = (block_ids >= 2 * q_blocks + v_blocks).astype(jnp.int32)
    return first + second + third


def butterfly_sum(x, axis):
    size = lax.axis_size(axis)
    for bit in range(size.bit_length() - 1):
        pairs = [(i, i ^ (1 << bit)) for i in range(size)]
        x = x + lax.ppermute(x, axis, pairs)
    return x


def doubling_gather(x, axis, bits):
    size = lax.axis_size(axis)
    for bit in bits:
        pairs = [(i, i ^ (1 << bit)) for i in range(size)]
        x = jnp.concatenate([x, lax.ppermute(x, axis, pairs)], axis=0)
    return x


def halving_sum(x, axis, bits):
    index = lax.axis_index(axis)
    size = lax.axis_size(axis)
    for bit in bits:
        half = x.shape[0] // 2
        upper = ((index >> bit) & 1) == 1
        keep = jnp.where(upper, x[half:], x[:half])
        send = jnp.where(upper, x[:half], x[half:])
        pairs = [(i, i ^ (1 << bit)) for i in range(size)]
        x = keep + lax.ppermute(send, axis, pairs)
    return x


def doubling_merge(x, axis, bits):
    index = lax.axis_index(axis)
    size = lax.axis_size(axis)
    for bit in bits:
        upper = ((index >> bit) & 1) == 1
        pairs = [(i, i ^ (1 << bit)) for i in range(size)]
        got = lax.ppermute(x, axis, pairs)
        x = jnp.where(upper, jnp.concatenate([got, x], axis=0), jnp.concatenate([x, got], axis=0))
    return x


def rounded_butterfly_sum(x, axis, bits):
    size = lax.axis_size(axis)
    for bit in bits:
        pairs = [(i, i ^ (1 << bit)) for i in range(size)]
        narrow = x.astype(jnp.bfloat16)
        x = narrow.astype(jnp.float32) + lax.ppermute(narrow, axis, pairs).astype(jnp.float32)
    return x


def owner_scatter(local_grad, slot_block, axis, orders):
    index = lax.axis_index(axis)
    size = lax.axis_size(axis)
    slots = slot_block.shape[0] // size
    count, rows, cols = local_grad.shape
    n_pieces = len(orders)
    part = rows // n_pieces
    flat = local_grad.reshape(count * n_pieces, part, cols)
    position = jnp.arange(size, dtype=jnp.int32)
    halves = []
    for k, order in enumerate(orders):
        steps = len(order)
        mask = sum(((position >> (steps - 1 - j)) & 1) << bit for j, bit in enumerate(order))
        dest = index ^ mask
        slot_index = (dest[:, None] * slots + jnp.arange(slots, dtype=jnp.int32)[None, :]).reshape(-1)
        source = jnp.take(slot_block, slot_index, mode="clip") * n_pieces + k
        middle = source.shape[0] // 2
        halves.append(
            (
                jnp.take(flat, source[:middle], axis=0, mode="clip"),
                jnp.take(flat, source[middle:], axis=0, mode="clip"),
            )
        )
    pieces = [None] * n_pieces
    for j in range(len(orders[0])):
        for k, order in enumerate(orders):
            if j == 0:
                keep, send = halves[k]
            else:
                x = pieces[k]
                middle = x.shape[0] // 2
                keep, send = x[:middle], x[middle:]
            pairs = [(i, i ^ (1 << order[j])) for i in range(size)]
            pieces[k] = keep + lax.ppermute(send, axis, pairs)
    return jnp.concatenate(pieces, axis=1)


def row_gather(x, axis):
    index = lax.axis_index(axis)
    size = lax.axis_size(axis)
    for bit in range(size.bit_length() - 1):
        upper = ((index >> bit) & 1) == 1
        pairs = [(i, i ^ (1 << bit)) for i in range(size)]
        got = lax.ppermute(x, axis, pairs)
        x = jnp.where(upper, jnp.concatenate([got, x], axis=1), jnp.concatenate([x, got], axis=1))
    return x


def local(partials, owner, basis_old, moment1, moment2, master):
    local_grad = partials[0]
    count = local_grad.shape[0]
    n_data = lax.axis_size("dp")
    slots = moment1.shape[0]
    total_slots = n_data * slots
    my_index = lax.axis_index("dp")
    block_ids = jnp.arange(count, dtype=jnp.int32)
    same_owner = owner[:, None] == owner[None, :]
    earlier = block_ids[None, :] < block_ids[:, None]
    rank_within = jnp.sum((same_owner & earlier).astype(jnp.int32), axis=1)
    slot_of = owner * slots + rank_within
    slot_ids = jnp.arange(total_slots, dtype=jnp.int32)
    slot_hits = slot_of[None, :] == slot_ids[:, None]
    filled = jnp.any(slot_hits, axis=1)
    slot_block = jnp.sum(jnp.where(slot_hits, block_ids[None, :], 0), axis=1)
    n_bits = n_data.bit_length() - 1
    if n_bits == 6:
        scatter_orders = [[0, 1, 3, 2, 4, 5], [0, 3, 1, 4, 2, 5]]
        gather_orders = [[5, 4, 2, 3, 1, 0], [5, 4, 2, 1, 3, 0]]
    else:
        scatter_orders = [list(range(n_bits)), list(range(n_bits))]
        gather_orders = [list(range(n_bits))[::-1], list(range(n_bits))[::-1]]
    owned_grad = owner_scatter(local_grad, slot_block, "dp", scatter_orders)
    my_blocks = lax.dynamic_slice_in_dim(slot_block, my_index * slots, slots)
    my_filled = lax.dynamic_slice_in_dim(filled, my_index * slots, slots)
    my_matrix = matrix_index(my_blocks)
    old_each = jnp.take(basis_old, my_matrix, axis=0, mode="clip")
    crossed = butterfly_sum(
        jnp.einsum("scd,sdr->scr", owned_grad, old_each, precision=HIGH), "sub"
    )
    refresh_term = jnp.einsum("scd,scr->sdr", owned_grad, crossed, precision=HIGH)
    matrix_hits = (
        (my_matrix[:, None] == jnp.arange(NMAT, dtype=jnp.int32)[None, :]) & my_filled[:, None]
    ).astype(jnp.float32)
    local_refresh = jnp.einsum("sm,sdr->mdr", matrix_hits, refresh_term, precision=HIGH)
    link_order = [0, 1, 3, 2, 4, 5] if n_bits == 6 else list(range(n_bits))
    flat_refresh = local_refresh.reshape(-1, local_refresh.shape[-1])
    refresh = doubling_merge(
        halving_sum(flat_refresh, "dp", link_order), "dp", link_order[::-1]
    ).reshape(local_refresh.shape)
    refresh_each = jnp.take(refresh, my_matrix, axis=0, mode="clip")
    n_mat, rows, rank = refresh.shape
    gram_part = jnp.einsum("mdr,mds->mrs", refresh, refresh, precision=HIGH)
    cross_part = jnp.einsum("scd,sdr->scr", owned_grad, refresh_each, precision=HIGH)
    sub_bits = list(range(lax.axis_size("sub").bit_length() - 1))
    split = n_mat // 2
    gram = jnp.concatenate(
        [
            rounded_butterfly_sum(gram_part[:split], "sub", sub_bits),
            rounded_butterfly_sum(gram_part[split:], "sub", sub_bits[::-1]),
        ],
        axis=0,
    )
    cross = butterfly_sum(cross_part, "sub")
    norm_sq = jnp.trace(gram, axis1=1, axis2=2) + NORM_EPS
    g0 = gram / norm_sq[:, None, None]
    eye = jnp.broadcast_to(jnp.eye(rank, dtype=jnp.float32), g0.shape)
    poly = 1.5 * eye - 0.5 * g0
    for sweep in range(1, NS_ITERS):
        inner = jnp.einsum("mst,mtu->msu", g0, poly, precision=SMALL)
        h = jnp.einsum("msr,msu->mru", poly, inner, precision=SMALL)
        poly = 1.5 * poly - 0.5 * jnp.einsum("mrs,msu->mru", poly, h, precision=SMALL)
    inv_norm = 1.0 / jnp.sqrt(norm_sq)
    basis = jnp.einsum("mdr,mrs->mds", refresh, poly, precision=HIGH) * inv_norm[:, None, None]
    new_each = jnp.take(basis, my_matrix, axis=0, mode="clip")
    poly_each = jnp.take(poly, my_matrix, axis=0, mode="clip")
    projected_all = jnp.einsum("scr,sru->scu", cross, poly_each, precision=HIGH) * jnp.take(
        inv_norm, my_matrix
    )[:, None, None]
    rows_here = moment1.shape[1]
    projected = lax.dynamic_slice_in_dim(
        projected_all, lax.axis_index("sub") * rows_here, rows_here, axis=1
    )
    first_new = BETA_ONE * moment1 + (1.0 - BETA_ONE) * projected
    second_new = BETA_TWO * moment2 + (1.0 - BETA_TWO) * projected * projected
    adam_step = first_new / CORR_ONE / (jnp.sqrt(second_new / CORR_TWO) + TINY)
    full_step = row_gather(adam_step.astype(jnp.bfloat16), "sub").astype(adam_step.dtype)
    update = jnp.einsum("scr,sdr->scd", full_step, new_each, precision=HIGH)
    new_master = (master.astype(jnp.float32) - LEARN * update).astype(jnp.bfloat16)
    apart = my_index ^ owner
    shared = 0
    while shared < n_bits and all(o[shared] == gather_orders[0][shared] for o in gather_orders):
        shared += 1
    common = doubling_gather(new_master, "dp", gather_orders[0][:shared])
    share = new_master.shape[1] // len(gather_orders)
    weight_parts = []
    for k, order in enumerate(gather_orders):
        every_slot = doubling_gather(common[:, k * share : (k + 1) * share], "dp", order[shared:])
        place = sum(((apart >> bit) & 1) << step for step, bit in enumerate(order))
        weight_parts.append(
            jnp.take(every_slot, place * slots + rank_within, axis=0, mode="clip")
        )
    weights = jnp.concatenate(weight_parts, axis=1)
    moment1_new = jnp.where(my_filled[:, None, None], first_new, 0.0)
    moment2_new = jnp.where(my_filled[:, None, None], second_new, 0.0)
    return (weights, basis, moment1_new, moment2_new)


def solution(mesh):
    return jax.shard_map(
        local,
        mesh=mesh,
        in_specs=(
            P("dp", None, None, "sub"),
            P(),
            P(None, "sub", None),
            P("dp", "sub", None),
            P("dp", "sub", None),
            P("dp", None, "sub"),
        ),
        out_specs=(
            P(None, None, "sub"),
            P(None, "sub", None),
            P("dp", "sub", None),
            P("dp", "sub", None),
        ),
        check_vma=False,
    )
```

```python
import jax
import jax.numpy as jnp
from jax import lax
from jax.sharding import PartitionSpec as P

D = 1024
VW = 2048
BW = 64
NS_ITERS = 5
NMAT = 4


HIGH = lax.Precision.HIGH
SMALL = lax.Precision.HIGH
BETA_ONE = 0.9
BETA_TWO = 0.999
CORR_ONE = 1.0 - 0.9**10
CORR_TWO = 1.0 - 0.999**10
LEARN = 0.05
TINY = 1e-08
NORM_EPS = 1e-06


def matrix_index(block_ids):
    q_blocks = D // BW
    v_blocks = VW // BW
    first = (block_ids >= q_blocks).astype(jnp.int32)
    second = (block_ids >= 2 * q_blocks).astype(jnp.int32)
    third = (block_ids >= 2 * q_blocks + v_blocks).astype(jnp.int32)
    return first + second + third


def butterfly_sum(x, axis):
    size = lax.axis_size(axis)
    for bit in range(size.bit_length() - 1):
        pairs = [(i, i ^ (1 << bit)) for i in range(size)]
        x = x + lax.ppermute(x, axis, pairs)
    return x


def doubling_gather(x, axis, bits):
    size = lax.axis_size(axis)
    for bit in bits:
        pairs = [(i, i ^ (1 << bit)) for i in range(size)]
        x = jnp.concatenate([x, lax.ppermute(x, axis, pairs)], axis=0)
    return x


def halving_sum(x, axis, bits):
    index = lax.axis_index(axis)
    size = lax.axis_size(axis)
    for bit in bits:
        half = x.shape[0] // 2
        upper = ((index >> bit) & 1) == 1
        keep = jnp.where(upper, x[half:], x[:half])
        send = jnp.where(upper, x[:half], x[half:])
        pairs = [(i, i ^ (1 << bit)) for i in range(size)]
        x = keep + lax.ppermute(send, axis, pairs)
    return x


def doubling_merge(x, axis, bits):
    index = lax.axis_index(axis)
    size = lax.axis_size(axis)
    for bit in bits:
        upper = ((index >> bit) & 1) == 1
        pairs = [(i, i ^ (1 << bit)) for i in range(size)]
        got = lax.ppermute(x, axis, pairs)
        x = jnp.where(upper, jnp.concatenate([got, x], axis=0), jnp.concatenate([x, got], axis=0))
    return x


def rounded_butterfly_sum(x, axis, bits):
    size = lax.axis_size(axis)
    for bit in bits:
        pairs = [(i, i ^ (1 << bit)) for i in range(size)]
        narrow = x.astype(jnp.bfloat16)
        x = narrow.astype(jnp.float32) + lax.ppermute(narrow, axis, pairs).astype(jnp.float32)
    return x


def owner_scatter(local_grad, slot_block, axis, orders):
    index = lax.axis_index(axis)
    size = lax.axis_size(axis)
    slots = slot_block.shape[0] // size
    count, rows, cols = local_grad.shape
    n_pieces = len(orders)
    part = rows // n_pieces
    flat = local_grad.reshape(count * n_pieces, part, cols)
    position = jnp.arange(size, dtype=jnp.int32)
    halves = []
    for k, order in enumerate(orders):
        steps = len(order)
        mask = sum(((position >> (steps - 1 - j)) & 1) << bit for j, bit in enumerate(order))
        dest = index ^ mask
        slot_index = (dest[:, None] * slots + jnp.arange(slots, dtype=jnp.int32)[None, :]).reshape(-1)
        source = jnp.take(slot_block, slot_index, mode="clip") * n_pieces + k
        middle = source.shape[0] // 2
        halves.append(
            (
                jnp.take(flat, source[:middle], axis=0, mode="clip"),
                jnp.take(flat, source[middle:], axis=0, mode="clip"),
            )
        )
    pieces = [None] * n_pieces
    steps = len(orders[0])
    merge_at = steps
    while merge_at > 1 and all(o[merge_at - 1] == orders[0][merge_at - 1] for o in orders):
        merge_at -= 1
    for j in range(steps):
        if j == merge_at and len(pieces) > 1:
            pieces = [jnp.concatenate(pieces, axis=1)]
            orders = orders[:1]
        for k, order in enumerate(orders):
            if j == 0:
                keep, send = halves[k]
            else:
                x = pieces[k]
                middle = x.shape[0] // 2
                keep, send = x[:middle], x[middle:]
            pairs = [(i, i ^ (1 << order[j])) for i in range(size)]
            pieces[k] = keep + lax.ppermute(send, axis, pairs)
    return jnp.concatenate(pieces, axis=1)


def row_gather(x, axis):
    index = lax.axis_index(axis)
    size = lax.axis_size(axis)
    for bit in range(size.bit_length() - 1):
        upper = ((index >> bit) & 1) == 1
        pairs = [(i, i ^ (1 << bit)) for i in range(size)]
        got = lax.ppermute(x, axis, pairs)
        x = jnp.where(upper, jnp.concatenate([got, x], axis=1), jnp.concatenate([x, got], axis=1))
    return x


def local(partials, owner, basis_old, moment1, moment2, master):
    local_grad = partials[0]
    count = local_grad.shape[0]
    n_data = lax.axis_size("dp")
    slots = moment1.shape[0]
    total_slots = n_data * slots
    my_index = lax.axis_index("dp")
    block_ids = jnp.arange(count, dtype=jnp.int32)
    same_owner = owner[:, None] == owner[None, :]
    earlier = block_ids[None, :] < block_ids[:, None]
    rank_within = jnp.sum((same_owner & earlier).astype(jnp.int32), axis=1)
    slot_of = owner * slots + rank_within
    slot_ids = jnp.arange(total_slots, dtype=jnp.int32)
    slot_hits = slot_of[None, :] == slot_ids[:, None]
    filled = jnp.any(slot_hits, axis=1)
    slot_block = jnp.sum(jnp.where(slot_hits, block_ids[None, :], 0), axis=1)
    n_bits = n_data.bit_length() - 1
    if n_bits == 6:
        scatter_orders = [[0, 1, 3, 2, 4, 5], [0, 3, 1, 2, 4, 5]]
        gather_orders = [[5, 4, 2, 3, 1, 0], [5, 4, 2, 1, 3, 0]]
    else:
        scatter_orders = [list(range(n_bits)), list(range(n_bits))]
        gather_orders = [list(range(n_bits))[::-1], list(range(n_bits))[::-1]]
    owned_grad = owner_scatter(local_grad, slot_block, "dp", scatter_orders)
    my_blocks = lax.dynamic_slice_in_dim(slot_block, my_index * slots, slots)
    my_filled = lax.dynamic_slice_in_dim(filled, my_index * slots, slots)
    my_matrix = matrix_index(my_blocks)
    old_each = jnp.take(basis_old, my_matrix, axis=0, mode="clip")
    crossed = butterfly_sum(
        jnp.einsum("scd,sdr->scr", owned_grad, old_each, precision=HIGH), "sub"
    )
    refresh_term = jnp.einsum("scd,scr->sdr", owned_grad, crossed, precision=HIGH)
    matrix_hits = (
        (my_matrix[:, None] == jnp.arange(NMAT, dtype=jnp.int32)[None, :]) & my_filled[:, None]
    ).astype(jnp.float32)
    local_refresh = jnp.einsum("sm,sdr->mdr", matrix_hits, refresh_term, precision=HIGH)
    link_order = [0, 1, 3, 2, 4, 5] if n_bits == 6 else list(range(n_bits))
    flat_refresh = local_refresh.reshape(-1, local_refresh.shape[-1])
    refresh = doubling_merge(
        halving_sum(flat_refresh, "dp", link_order), "dp", link_order[::-1]
    ).reshape(local_refresh.shape)
    refresh_each = jnp.take(refresh, my_matrix, axis=0, mode="clip")
    n_mat, rows, rank = refresh.shape
    gram_part = jnp.einsum("mdr,mds->mrs", refresh, refresh, precision=HIGH)
    cross_part = jnp.einsum("scd,sdr->scr", owned_grad, refresh_each, precision=HIGH)
    sub_bits = list(range(lax.axis_size("sub").bit_length() - 1))
    split = n_mat // 2
    gram = jnp.concatenate(
        [
            rounded_butterfly_sum(gram_part[:split], "sub", sub_bits),
            rounded_butterfly_sum(gram_part[split:], "sub", sub_bits[::-1]),
        ],
        axis=0,
    )
    cross = butterfly_sum(cross_part, "sub")
    norm_sq = jnp.trace(gram, axis1=1, axis2=2) + NORM_EPS
    g0 = gram / norm_sq[:, None, None]
    eye = jnp.broadcast_to(jnp.eye(rank, dtype=jnp.float32), g0.shape)
    poly = 1.5 * eye - 0.5 * g0
    for sweep in range(1, NS_ITERS):
        inner = jnp.einsum("mst,mtu->msu", g0, poly, precision=SMALL)
        h = jnp.einsum("msr,msu->mru", poly, inner, precision=SMALL)
        poly = 1.5 * poly - 0.5 * jnp.einsum("mrs,msu->mru", poly, h, precision=SMALL)
    inv_norm = 1.0 / jnp.sqrt(norm_sq)
    basis = jnp.einsum("mdr,mrs->mds", refresh, poly, precision=HIGH) * inv_norm[:, None, None]
    new_each = jnp.take(basis, my_matrix, axis=0, mode="clip")
    poly_each = jnp.take(poly, my_matrix, axis=0, mode="clip")
    projected_all = jnp.einsum("scr,sru->scu", cross, poly_each, precision=HIGH) * jnp.take(
        inv_norm, my_matrix
    )[:, None, None]
    rows_here = moment1.shape[1]
    projected = lax.dynamic_slice_in_dim(
        projected_all, lax.axis_index("sub") * rows_here, rows_here, axis=1
    )
    first_new = BETA_ONE * moment1 + (1.0 - BETA_ONE) * projected
    second_new = BETA_TWO * moment2 + (1.0 - BETA_TWO) * projected * projected
    adam_step = first_new / CORR_ONE / (jnp.sqrt(second_new / CORR_TWO) + TINY)
    full_step = row_gather(adam_step.astype(jnp.bfloat16), "sub").astype(adam_step.dtype)
    update = jnp.einsum("scr,sdr->scd", full_step, new_each, precision=HIGH)
    new_master = (master.astype(jnp.float32) - LEARN * update).astype(jnp.bfloat16)
    apart = my_index ^ owner
    shared = 0
    while shared < n_bits and all(o[shared] == gather_orders[0][shared] for o in gather_orders):
        shared += 1
    common = doubling_gather(new_master, "dp", gather_orders[0][:shared])
    share = new_master.shape[1] // len(gather_orders)
    weight_parts = []
    for k, order in enumerate(gather_orders):
        every_slot = doubling_gather(common[:, k * share : (k + 1) * share], "dp", order[shared:])
        place = sum(((apart >> bit) & 1) << step for step, bit in enumerate(order))
        weight_parts.append(
            jnp.take(every_slot, place * slots + rank_within, axis=0, mode="clip")
        )
    weights = jnp.concatenate(weight_parts, axis=1)
    moment1_new = jnp.where(my_filled[:, None, None], first_new, 0.0)
    moment2_new = jnp.where(my_filled[:, None, None], second_new, 0.0)
    return (weights, basis, moment1_new, moment2_new)


def solution(mesh):
    return jax.shard_map(
        local,
        mesh=mesh,
        in_specs=(
            P("dp", None, None, "sub"),
            P(),
            P(None, "sub", None),
            P("dp", "sub", None),
            P("dp", "sub", None),
            P("dp", None, "sub"),
        ),
        out_specs=(
            P(None, None, "sub"),
            P(None, "sub", None),
            P("dp", "sub", None),
            P("dp", "sub", None),
        ),
        check_vma=False,
    )
```
